32 devices in a mesh: phi: 4 (over y, core), eta: 8 (over z, x).
Axes of the slice: x: 2, y: 2, z: 4, core: 2. Of those that a mesh axis runs over, the one named last changes fastest.
Arguments:
- edges: bfloat16 [65536, 128], P(('phi', 'eta')), may hold values from -6 to 6
- cotangent: bfloat16 [65536, 128], P(('phi', 'eta')), may hold values from -6 to 6
- send_rows: int32 [32, 32, 32], P(('phi', 'eta')), may hold values from 0 to 2047
- send_count: int32 [32, 32], P(('phi', 'eta')), may hold values from 1 to 32, as said below
- trip_local: int32 [262144], P(('phi', 'eta')), may hold values from 0 to 2047
- trip_remote: int32 [262144], P(('phi', 'eta')), may hold values from 0 to 1023, as said below
- w_first: bfloat16 [384, 256], replicated, may hold values from -0.3125 to 0.3125
- bias_first: float32 [256], replicated, may hold values from -4 to 4
- w_second: bfloat16 [256, 128], replicated, may hold values from -0.375 to 0.375
Outputs:
- new_edges: bfloat16 [65536, 128], P(('phi', 'eta'))
- edge_grad: bfloat16 [65536, 128], P(('phi', 'eta'))
- grad_first: float32 [384, 256], replicated
- grad_bias: float32 [256], replicated
- grad_second: float32 [256, 128], replicated
The draws below stay inside these ranges and needn't reach their ends.
Inputs may be any that keep to these rules, and one draw needn't show every extreme that they name: `send_count`: some destination device has every slot live from every source. `trip_remote`: each triplet names a live slot of a source device toward its own owner.
All inputs are finite; a program needn't handle non-finite values.
Results may differ from the reference program's by a relative error of at most 0.0053.
Values may be sent and summed in bfloat16 or wider, within the bound.
A program may use at most 128 MiB of HBM per device.

```python
import jax
import jax.numpy as jnp
from jax import lax

F = 128
HID = 256
EDGE_DEV = 2048
TRIP_DEV = 8192
CAP = 32
NDEV = 32
IN = 384
EDGES = 65536
TRIPLETS = 262144


def shared_counts(key):
    first = jax.random.fold_in(key, 7)
    second = jax.random.fold_in(key, 8)
    counts = jax.random.randint(first, (NDEV, NDEV), 1, CAP + 1)
    fullest = jax.random.randint(second, (), 0, NDEV)
    counts = jnp.where(jnp.arange(NDEV)[None, :] == fullest, CAP, counts)
    return (counts.astype(jnp.int32), fullest)


def draw_send_count(key, part):
    counts, fullest = shared_counts(key)
    return counts


def draw_trip_remote(key, part):
    counts, fullest = shared_counts(key)
    source = jax.random.randint(jax.random.fold_in(key, 11), (TRIPLETS,), 0, NDEV)
    spread = jax.random.randint(jax.random.fold_in(key, 12), (TRIPLETS,), 0, 1048576)
    position = jnp.arange(TRIPLETS)
    owner = position // TRIP_DEV
    live_count = counts[source, owner]
    slot = spread % live_count
    picked = source * CAP + slot
    picked = jnp.where(position == fullest * TRIP_DEV, 0, picked)
    picked = jnp.where(position == fullest * TRIP_DEV + TRIP_DEV - 1, NDEV * CAP - 1, picked)
    return picked.astype(jnp.int32)


def with_ends(drawn, rng, smallest, high):
    shape = drawn.shape
    index_at = [jax.random.randint(jax.random.fold_in(rng, axis), (), 0, shape[axis]) for axis in range(len(shape))]
    drawn = drawn.at[tuple(index_at)].set(smallest)
    longest = shape.index(max(shape))
    index_at[longest] = (index_at[longest] + 1) % shape[longest]
    return drawn.at[tuple(index_at)].set(high)


def block_scale(rng, extent, pieces, low, largest):
    def one(axis_at, parts):
        steps = jax.random.uniform(jax.random.fold_in(jax.random.fold_in(rng, 6), axis_at), (parts,), jnp.float32, low / len(pieces), largest / len(pieces))
        return jnp.repeat(jnp.exp(steps), extent[axis_at] // parts).reshape((-1,) + (1,) * (len(extent) - axis_at - 1))

    factor_of = one(*pieces[0])
    for cut in pieces[1:]:
        factor_of = factor_of * one(*cut)
    return factor_of


def scatter_about(rng, dims, scale, reach, split=(), kind=jnp.bfloat16):
    drawn = jax.random.normal(rng, dims, jnp.float32) * scale
    if len(split) > 0:
        drawn = block_scale(rng, dims, split, -0.22, 0.18) * drawn
    return jnp.clip(drawn, min=-reach, max=reach).astype(kind)


def setup_inputs(seed: int = 0) -> dict:
    keys = jax.random.split(jax.random.key(seed), 10)
    edges = scatter_about(keys[0], (EDGES, F), 1.0, 6.0, ((0, 32),))
    cotangent = scatter_about(keys[1], (EDGES, F), 1.0, 6.0, ((0, 32),))
    send_rows = with_ends(jax.random.randint(keys[2], (NDEV, NDEV, CAP), 0, EDGE_DEV), jax.random.fold_in(keys[2], 1), 0, EDGE_DEV - 1).astype(jnp.int32)
    send_count = draw_send_count(jax.random.fold_in(keys[9], 71), 0)
    trip_local = with_ends(jax.random.randint(keys[4], (TRIPLETS,), 0, EDGE_DEV), jax.random.fold_in(keys[4], 1), 0, EDGE_DEV - 1).astype(jnp.int32)
    trip_remote = draw_trip_remote(jax.random.fold_in(keys[9], 71), 0)
    w_first = scatter_about(keys[6], (IN, HID), IN ** -0.5, 0.3125)
    bias_first = scatter_about(keys[7], (HID,), 0.7, 4.0, (), jnp.float32)
    w_second = scatter_about(keys[8], (HID, F), HID ** -0.5, 0.375)
    return {"edges": edges, "cotangent": cotangent, "send_rows": send_rows, "send_count": send_count, "trip_local": trip_local, "trip_remote": trip_remote, "w_first": w_first, "bias_first": bias_first, "w_second": w_second}


def silu_slope(pre):
    sig = jax.nn.sigmoid(pre)
    return sig * (1.0 + pre * (1.0 - sig))


def owner_terms(owner, edges, cotangent, send_rows, send_count, trip_local, trip_remote, w_first, bias_first, w_second):
    rows = send_rows[:, owner, :]
    live = jnp.arange(CAP, dtype=jnp.int32)[None, :] < send_count[:, owner][:, None]
    global_rows = (jnp.arange(NDEV, dtype=jnp.int32)[:, None] * EDGE_DEV + rows).astype(jnp.int32)
    zero = jnp.zeros((), jnp.bfloat16)
    far_lat = jnp.where(live[:, :, None], edges[global_rows], zero).reshape(NDEV * CAP, F)
    far_cot = jnp.where(live[:, :, None], cotangent[global_rows], zero).reshape(NDEV * CAP, F)
    base = (owner * EDGE_DEV).astype(jnp.int32)
    own_lat = lax.dynamic_slice_in_dim(edges, base, EDGE_DEV, 0)
    own_cot = lax.dynamic_slice_in_dim(cotangent, base, EDGE_DEV, 0)
    tstart = (owner * TRIP_DEV).astype(jnp.int32)
    local_idx = lax.dynamic_slice_in_dim(trip_local, tstart, TRIP_DEV, 0)
    remote_idx = lax.dynamic_slice_in_dim(trip_remote, tstart, TRIP_DEV, 0)
    inner = own_lat[local_idx]
    inner_cot = own_cot[local_idx]
    outer = far_lat[remote_idx]
    outer_cot = far_cot[remote_idx]
    inner_f = inner.astype(jnp.float32)
    outer_f = outer.astype(jnp.float32)
    prod = (inner_f * outer_f).astype(jnp.bfloat16)
    joined = jnp.concatenate([inner, outer, prod], axis=1)
    pre = jnp.dot(joined, w_first, preferred_element_type=jnp.float32) + bias_first
    hidden = jax.nn.silu(pre).astype(jnp.bfloat16)
    message = jnp.dot(hidden, w_second, preferred_element_type=jnp.float32)
    local_msg = jax.ops.segment_sum(message, local_idx, EDGE_DEV)
    slot_msg = jax.ops.segment_sum(message, remote_idx, NDEV * CAP)
    dmsg = (inner_cot.astype(jnp.float32) + outer_cot.astype(jnp.float32)).astype(jnp.bfloat16)
    grad_second = jnp.dot(hidden.T, dmsg, preferred_element_type=jnp.float32)
    dpre = jnp.dot(dmsg, w_second.T, preferred_element_type=jnp.float32) * silu_slope(pre)
    dpre_b = dpre.astype(jnp.bfloat16)
    grad_first = jnp.dot(joined.T, dpre_b, preferred_element_type=jnp.float32)
    grad_bias = jnp.sum(dpre, axis=0)
    dx = jnp.dot(dpre_b, w_first.T, preferred_element_type=jnp.float32)
    d_inner = dx[:, :F] + dx[:, 2 * F:] * outer_f
    d_outer = dx[:, F:2 * F] + dx[:, 2 * F:] * inner_f
    local_grad = jax.ops.segment_sum(d_inner, local_idx, EDGE_DEV)
    slot_grad = jax.ops.segment_sum(d_outer, remote_idx, NDEV * CAP)
    slots = jnp.stack([slot_msg, slot_grad], axis=1).astype(jnp.bfloat16).reshape(NDEV, CAP, 2, F)
    slots = jnp.where(live[:, :, None, None], slots, zero)
    return base, global_rows, local_msg, local_grad, slots, grad_first, grad_bias, grad_second


def reference(edges, cotangent, send_rows, send_count, trip_local, trip_remote, w_first, bias_first, w_second):
    def step(carry, owner):
        msg_total, grad_total, acc_first, acc_bias, acc_second = carry
        base, global_rows, local_msg, local_grad, slots, g_first, g_bias, g_second = owner_terms(
            owner, edges, cotangent, send_rows, send_count, trip_local, trip_remote, w_first, bias_first, w_second)
        own_rows = base + jnp.arange(EDGE_DEV, dtype=jnp.int32)
        flat_rows = global_rows.reshape(-1)
        msg_total = msg_total.at[own_rows].add(local_msg)
        msg_total = msg_total.at[flat_rows].add(slots[:, :, 0, :].astype(jnp.float32).reshape(-1, F))
        grad_total = grad_total.at[own_rows].add(local_grad)
        grad_total = grad_total.at[flat_rows].add(slots[:, :, 1, :].astype(jnp.float32).reshape(-1, F))
        return (msg_total, grad_total, acc_first + g_first, acc_bias + g_bias, acc_second + g_second), None

    start = (jnp.zeros((EDGES, F), jnp.float32), jnp.zeros((EDGES, F), jnp.float32),
             jnp.zeros((IN, HID), jnp.float32), jnp.zeros((HID,), jnp.float32), jnp.zeros((HID, F), jnp.float32))
    final, _ = lax.scan(step, start, jnp.arange(NDEV, dtype=jnp.int32))
    msg_total, grad_total, grad_first, grad_bias, grad_second = final
    new_edges = (edges.astype(jnp.float32) + msg_total).astype(jnp.bfloat16)
    edge_grad = (cotangent.astype(jnp.float32) + grad_total).astype(jnp.bfloat16)
    return (new_edges, edge_grad, grad_first, grad_bias, grad_second)
```

```python
import functools

import jax
import jax.numpy as jnp
from jax import lax
from jax.experimental import pallas as pl
from jax.experimental.pallas import tpu as pltpu
from jax.sharding import PartitionSpec as P

AXES = ("phi", "eta")
F32 = jnp.float32
BF16 = jnp.bfloat16
I32 = jnp.int32
VMEM_LIMIT = 60 * 1024 * 1024
MESH = pl.DeviceIdType.MESH
WINDOW = 256
TILE = 512


def dot(a, b):
    return jnp.dot(a, b, preferred_element_type=F32)


def dot_nt(a, b):
    return lax.dot_general(a, b, (((1,), (1,)), ((), ())), preferred_element_type=F32)


def dot_tn(a, b):
    return lax.dot_general(a, b, (((0,), (0,)), ((), ())), preferred_element_type=F32)


def pick_rows(idx, n):
    t = idx.shape[1]
    cols = jnp.broadcast_to(idx, (128, t)).T
    lane = lax.broadcasted_iota(I32, (t, 128), 1)
    parts = [jnp.where(cols - 128 * j == lane, 1.0, 0.0).astype(BF16) for j in range(n // 128)]
    return jnp.concatenate(parts, axis=1)


def pick_cols(idx, n):
    row = lax.broadcasted_iota(I32, (n, idx.shape[1]), 0)
    return jnp.where(row == idx, 1.0, 0.0).astype(BF16)


def group_sort(x):
    g = x.shape[0]
    gb = g.bit_length() - 1
    n_bits = gb + 10
    lane = lax.broadcasted_iota(I32, (1, 8, 128), 2)
    sub = lax.broadcasted_iota(I32, (1, 8, 128), 1)
    grp = lax.broadcasted_iota(I32, (g, 8, 128), 0)

    def low(b):
        if b < gb:
            return (grp & (1 << b)) == 0
        if b < gb + 3:
            return (sub & (1 << (b - gb))) == 0
        return (lane & (1 << (b - gb - 3))) == 0

    for k in range(1, n_bits + 1):
        last = k == n_bits
        for j in range(k - 1, -1, -1):
            if last and j < gb + 3:
                break
            if j < gb:
                h = 1 << j
                split = (g // (2 * h), 2, h, 8, 128)
                y = x.reshape(split)
                a, b = y[:, 0], y[:, 1]
                small, large = jnp.minimum(a, b), jnp.maximum(a, b)
                up = low(k)
                if k < gb:
                    up = jnp.broadcast_to(up, (g, 8, 128)).reshape(split)[:, 0]
                else:
                    up = jnp.broadcast_to(up[None], a.shape)
                pair = [jnp.where(up, small, large), jnp.where(up, large, small)]
                x = jnp.stack(pair, axis=1).reshape(g, 8, 128)
            else:
                if j < gb + 3:
                    d, ax, size = 1 << (j - gb), 1, 8
                else:
                    d, ax, size = 1 << (j - gb - 3), 2, 128
                lo = low(j)
                if 2 * d == size:
                    other = pltpu.roll(x, d, ax)
                else:
                    other = jnp.where(
                        jnp.broadcast_to(lo, x.shape), pltpu.roll(x, size - d, ax), pltpu.roll(x, d, ax)
                    )
                take = lo if last else lo == low(k)
                x = jnp.where(
                    jnp.broadcast_to(take, x.shape), jnp.minimum(x, other), jnp.maximum(x, other)
                )
    return x


def place(n_phi, n_eta):
    phi = lax.axis_index("phi")
    eta = lax.axis_index("eta")
    return phi, eta, phi * n_eta + eta, n_phi * n_eta


def greet_all(n_eta, me, ndev):
    barrier = pltpu.get_barrier_semaphore()

    def greet(k, carry):
        peer = lax.rem(me + k, ndev)
        pl.semaphore_signal(
            barrier, inc=1, device_id=(peer // n_eta, lax.rem(peer, n_eta)), device_id_type=MESH
        )
        return carry

    lax.fori_loop(1, ndev, greet, 0)
    return barrier


def each(first, end, act):
    def body(k, carry):
        act(k)
        return carry

    lax.fori_loop(first, end, body, 0)


def slot_copy(n_phi, n_eta, k, src, dst, send_sem, recv_sem):
    phi, eta, me, ndev = place(n_phi, n_eta)
    to_phi, to_eta = lax.rem(phi + k // n_eta, n_phi), lax.rem(eta + lax.rem(k, n_eta), n_eta)
    return pltpu.make_async_remote_copy(
        src_ref=src.at[to_phi * n_eta + to_eta],
        dst_ref=dst.at[me],
        send_sem=send_sem.at[k],
        recv_sem=recv_sem.at[k],
        device_id=(to_phi, to_eta),
        device_id_type=MESH,
    )


def send_kernel(
    n_phi, n_eta, stride, rows_ref, count_ref, edges_ref, cot_ref, loc_ref, rem_ref,
    arr_ref, keys_ref, bounds_ref, flat_ref,
    outbox, inbox, send_sem, recv_sem,
):
    phi, eta, me, ndev = place(n_phi, n_eta)
    cap = rows_ref.shape[2]
    width = edges_ref.shape[1]
    barrier = greet_all(n_eta, me, ndev)
    copy_of = lambda k: slot_copy(n_phi, n_eta, k, outbox, inbox, send_sem, recv_sem)

    src = lax.broadcasted_iota(I32, (ndev, ndev), 0)
    dst = lax.broadcasted_iota(I32, (ndev, ndev), 1)
    counts = jnp.sum(jnp.where(src == dst, count_ref[...], 0), axis=1, keepdims=True)
    slot = lax.broadcasted_iota(I32, (ndev, cap), 1)
    live = jnp.where(slot < counts, rows_ref[0], -1)
    for d in range(ndev):
        flat_ref[:, d * cap : (d + 1) * cap] = live[d : d + 1, :]

    both = jnp.concatenate([edges_ref[...], cot_ref[...]], axis=1)
    part = n_eta * cap
    for p in range(n_phi):
        rows = flat_ref[:, p * part : (p + 1) * part]
        picked = dot(pick_rows(rows, edges_ref.shape[0]), both).astype(BF16)
        outbox[p * n_eta : (p + 1) * n_eta] = picked.reshape(n_eta, cap, 2 * width)
    inbox[me] = outbox[me]
    pl.semaphore_wait(barrier, ndev - 1)
    each(1, ndev, lambda k: copy_of(k).start())

    key = group_sort((loc_ref[...] * stride + rem_ref[...]).astype(F32)).astype(I32)
    group = key.shape[0] * 8
    flat_key = key.reshape(group, 128)
    loc = flat_key // stride
    bounds_ref[0:1, :] = jnp.min(loc, axis=0, keepdims=True)
    bounds_ref[1:2, :] = jnp.max(loc, axis=0, keepdims=True)
    by_group = flat_key.T
    per = keys_ref.shape[2] // group
    for l in range(128):
        keys_ref[l // per, :, l % per * group : (l % per + 1) * group] = by_group[l : l + 1, :]

    each(1, ndev, lambda k: copy_of(k).wait())
    arr_ref[...] = inbox[...].reshape(arr_ref.shape)


def main_kernel(
    fused, stride, bounds_ref, key_ref, edges_ref, cot_ref, arr_ref, w1_ref, b1_ref, w2_ref,
    sum_ref, slot_ref, grad_ref, bias_ref,
    near, mda, acc_r, g1, g2,
):
    step = pl.program_id(0)
    width = w2_ref.shape[1]
    n_edges = edges_ref.shape[0]
    slots_n = arr_ref.shape[0]

    @pl.when(step == 0)
    def _():
        sum_ref[...] = jnp.zeros_like(sum_ref)
        acc_r[...] = jnp.zeros_like(acc_r)
        g1[...] = jnp.zeros_like(g1)
        g2[...] = jnp.zeros_like(g2)
        bias_ref[...] = jnp.zeros_like(bias_ref)

    window = min(WINDOW, n_edges)
    per = bounds_ref.shape[1] // pl.num_programs(0)
    base = bounds_ref[0, step * per] // 16 * 16
    top = bounds_ref[1, step * per + per - 1]
    windows = (top - base) // window + 1
    key = key_ref[0]
    loc = key // stride
    rem = key - loc * stride

    def start_of(w):
        return pl.multiple_of(jnp.minimum(base + w * window, n_edges - window), 16)

    def rows_in(w):
        return jnp.where(loc >= base + w * window, loc - start_of(w), -1)

    def gather(w):
        span = pl.ds(start_of(w), window)
        rows = jnp.concatenate([edges_ref[span, :], cot_ref[span, :]], axis=1)
        return dot(pick_rows(rows_in(w), window), rows).astype(BF16)

    def scatter(w):
        sum_ref[pl.ds(start_of(w), window), :] += dot(pick_cols(rows_in(w), window), mda[...])

    near[...] = gather(0)

    @pl.when(windows > 1)
    def _():
        def more(w, carry):
            near[...] += gather(w)
            return carry

        lax.fori_loop(1, windows, more, 0)

    far = dot(pick_rows(rem, slots_n), arr_ref[...])
    a_b = near[:, :width]
    a = a_b.astype(F32)
    b = far[:, :width]
    dm = (near[:, width:].astype(F32) + far[:, width:]).astype(BF16)
    x = jnp.concatenate([a_b, b.astype(BF16), (a * b).astype(BF16)], axis=1)
    pre = dot(x, w1_ref[...]) + b1_ref[...]
    sig = 0.5 * jnp.tanh(0.5 * pre) + 0.5
    h = (pre * sig).astype(BF16)
    m = dot(h, w2_ref[...]).astype(BF16)
    dpre = dot_nt(dm, w2_ref[...]) * (sig * (1.0 + pre * (1.0 - sig)))
    dpre_b = dpre.astype(BF16)
    dx = dot_nt(dpre_b, w1_ref[...])
    dprod = dx[:, 2 * width :]
    mda[:, :width] = m
    mda[:, width:] = (dx[:, :width] + dprod * b).astype(BF16)
    db = (dx[:, width : 2 * width] + dprod * a).astype(BF16)
    g1[...] += dot_tn(x, dpre_b)
    g2[...] += dot_tn(h, dm)
    bias_ref[...] += jnp.sum(dpre, axis=0, keepdims=True)
    acc_r[...] += dot(pick_cols(rem, slots_n), jnp.concatenate([m, db], axis=1))
    scatter(0)

    @pl.when(windows > 1)
    def _():
        def more(w, carry):
            scatter(w)
            return carry

        lax.fori_loop(1, windows, more, 0)

    @pl.when(step == pl.num_programs(0) - 1)
    def _():
        second = jnp.concatenate(
            [g2[k * width : (k + 1) * width, :] for k in range(g2.shape[0] // width)], axis=1
        )
        slot_ref[...] = acc_r[...].astype(BF16)
        n_in = g1.shape[0]
        grad_ref[:n_in, :] = g1[...].astype(BF16)
        grad_ref[n_in:, :] = second.astype(BF16)


def back_kernel(
    n_phi, n_eta, n_hi, flat_ref, near_ref, edges_ref, cot_ref, pay_ref, pack_ref, bias_ref,
    new_ref, grad_ref, g1_ref, g2_ref, gb_ref,
    inbox, total, plane_in, line_in, line_out, plane_out, biases,
    send_s, recv_s, send_g, recv_g, send_b, recv_b,
):
    phi, eta, me, ndev = place(n_phi, n_eta)
    cap, wide = inbox.shape[1:]
    width = edges_ref.shape[1]
    n_lo = n_eta // n_hi
    n_plane = n_phi * n_lo
    hi, lo = eta // n_lo, lax.rem(eta, n_lo)
    my_plane = phi * n_lo + lo
    barrier = greet_all(n_eta, me, ndev)

    def in_plane(k):
        other = lax.rem(my_plane + k, n_plane)
        return other, (other // n_lo, hi * n_lo + lax.rem(other, n_lo))

    def in_line(k):
        other = lax.rem(hi + k, n_hi)
        return other, (phi, other * n_lo + lo)

    def grad_copy(slot, src, dst, peer):
        return pltpu.make_async_remote_copy(
            src_ref=src, dst_ref=dst, send_sem=send_g.at[slot], recv_sem=recv_g.at[slot],
            device_id=peer, device_id_type=MESH,
        )

    def plane_reduce(k):
        other, peer = in_plane(k)
        return grad_copy(k, pack_ref.at[other], plane_in.at[my_plane], peer)

    def line_reduce(k):
        other, peer = in_line(k)
        return grad_copy(n_plane + k, line_in.at[n_hi + other], line_in.at[hi], peer)

    def line_gather(k):
        other, peer = in_line(k)
        return grad_copy(n_plane + n_hi + k, line_out.at[hi], line_out.at[hi], peer)

    def plane_gather(k):
        other, peer = in_plane(k)
        return grad_copy(
            n_plane + 2 * n_hi + k, plane_out.at[my_plane], plane_out.at[my_plane], peer
        )

    def bias_copy(k):
        peer = lax.rem(me + k, ndev)
        return pltpu.make_async_remote_copy(
            src_ref=biases.at[me], dst_ref=biases.at[me], send_sem=send_b.at[k], recv_sem=recv_b.at[k],
            device_id=(peer // n_eta, lax.rem(peer, n_eta)), device_id_type=MESH,
        )

    copy_of = lambda k: slot_copy(n_phi, n_eta, k, pay_ref, inbox, send_s, recv_s)

    biases[me] = bias_ref[...]
    plane_in[my_plane] = pack_ref[my_plane]
    inbox[me] = pay_ref[me]
    pl.semaphore_wait(barrier, ndev - 1)
    each(1, n_plane, lambda k: plane_reduce(k).start())
    each(1, ndev, lambda k: copy_of(k).start())
    each(1, ndev, lambda k: bias_copy(k).start())

    each(1, n_plane, lambda k: plane_reduce(k).wait())
    line_in[n_hi:] = jnp.sum(plane_in[...].astype(F32), axis=0).astype(BF16)
    line_in[hi] = line_in[n_hi + hi]
    each(1, n_hi, lambda k: line_reduce(k).start())

    part = n_eta * cap

    def add(q):
        group = lax.rem(phi + n_phi - q, n_phi)
        rows = flat_ref[group]
        data = inbox[pl.ds(group * n_eta, n_eta)].reshape(part, wide)
        return dot(pick_cols(rows, edges_ref.shape[0]), data)

    each(1, n_eta, lambda k: copy_of(k).wait())
    total[...] = near_ref[...] + add(0)
    each(1, n_hi, lambda k: line_reduce(k).wait())
    line_out[hi] = jnp.sum(line_in[:n_hi].astype(F32), axis=0).astype(BF16)
    each(1, n_hi, lambda k: line_gather(k).start())
    for q in range(1, n_phi):
        each(q * n_eta, (q + 1) * n_eta, lambda k: copy_of(k).wait())
        total[...] += add(q)
        if q == 1:
            each(1, n_hi, lambda k: line_gather(k).wait())
            plane_out[my_plane] = line_out[...]
            each(1, n_plane, lambda k: plane_gather(k).start())
    new_ref[...] = (edges_ref[...].astype(F32) + total[:, :width]).astype(BF16)
    grad_ref[...] = (cot_ref[...].astype(F32) + total[:, width:]).astype(BF16)
    each(1, ndev, lambda k: bias_copy(k).wait())
    gb_ref[...] = jnp.sum(biases[...], axis=0)
    each(1, n_plane, lambda k: plane_gather(k).wait())
    share = plane_out.shape[1] * plane_out.shape[2]
    n_in = g1_ref.shape[0]
    hid = plane_out.shape[3]
    pack = plane_out[...].astype(F32).reshape(n_plane * share, hid)
    g1_ref[...] = pack[:n_in]
    for k in range(g2_ref.shape[0] // width):
        g2_ref[k * width : (k + 1) * width, :] = pack[n_in:, k * width : (k + 1) * width]


def hand_kernel(*refs):
    n = (len(refs) - 1) // 2
    copies = [pltpu.make_async_copy(refs[i], refs[n + i], refs[-1].at[i]) for i in range(n)]
    for copy in copies:
        copy.start()
    for copy in copies:
        copy.wait()


def full(shape):
    return pl.BlockSpec(shape, lambda i: (0,) * len(shape))


def local(
    edges, cotangent, send_rows, send_count, trip_local, trip_remote, w_first, bias_first, w_second
):
    n_edges, width = edges.shape
    n_in, hid = w_first.shape
    n_phi, n_eta = lax.axis_size("phi"), lax.axis_size("eta")
    ndev = n_phi * n_eta
    cap = send_rows.shape[2]
    slots = ndev * cap
    n_trip = trip_local.shape[0]
    wide = 2 * width
    pack = n_in + width
    stride = 1 << (slots - 1).bit_length()
    tile = min(TILE, n_trip)
    steps = n_trip // tile
    box = (ndev, cap, wide)
    whole = pl.BlockSpec(memory_space=pltpu.VMEM)
    remote = lambda n: pltpu.CompilerParams(
        collective_id=n, has_side_effects=True, vmem_limit_bytes=VMEM_LIMIT
    )
    each_dev = pltpu.SemaphoreType.DMA((ndev,))
    arrived, keys, bounds, flat = pl.pallas_call(
        functools.partial(send_kernel, n_phi, n_eta, stride),
        in_specs=[whole] * 6,
        out_specs=[whole] * 4,
        out_shape=[
            jax.ShapeDtypeStruct((slots, wide), BF16),
            jax.ShapeDtypeStruct((steps, 1, tile), I32),
            jax.ShapeDtypeStruct((2, 128), I32),
            jax.ShapeDtypeStruct((1, slots), I32),
        ],
        scratch_shapes=[pltpu.VMEM(box, BF16), pltpu.VMEM(box, BF16), each_dev, each_dev],
        compiler_params=remote(0),
        name="send_rows",
    )(
        send_rows, send_count, edges, cotangent,
        trip_local.reshape(n_trip // 1024, 8, 128), trip_remote.reshape(n_trip // 1024, 8, 128),
    )

    near_sum, payload, grads, bias = pl.pallas_call(
        functools.partial(main_kernel, False, stride),
        grid=(steps,),
        in_specs=[
            pl.BlockSpec(memory_space=pltpu.SMEM),
            pl.BlockSpec((1, 1, tile), lambda i: (i, 0, 0)),
            full((n_edges, width)),
            full((n_edges, width)),
            full((slots, wide)),
            full((n_in, hid)),
            full((1, hid)),
            full((hid, width)),
        ],
        out_specs=[full((n_edges, wide)), full((slots, wide)), full((pack, hid)), full((1, hid))],
        out_shape=[
            jax.ShapeDtypeStruct((n_edges, wide), F32),
            jax.ShapeDtypeStruct((slots, wide), BF16),
            jax.ShapeDtypeStruct((pack, hid), BF16),
            jax.ShapeDtypeStruct((1, hid), F32),
        ],
        scratch_shapes=[
            pltpu.VMEM((tile, wide), BF16),
            pltpu.VMEM((tile, wide), BF16),
            pltpu.VMEM((slots, wide), F32),
            pltpu.VMEM((n_in, hid), F32),
            pltpu.VMEM((hid, width), F32),
        ],
        compiler_params=pltpu.CompilerParams(
            dimension_semantics=("arbitrary",), vmem_limit_bytes=VMEM_LIMIT
        ),
        name="triplets",
    )(bounds, keys, edges, cotangent, arrived, w_first, bias_first.reshape(1, hid), w_second)

    n_hi = 4 if n_eta % 4 == 0 else 1
    n_plane = ndev // n_hi
    shard = (n_hi, pack // ndev, hid)
    grad_sems = pltpu.SemaphoreType.DMA((2 * n_plane + 2 * n_hi,))
    outs = pl.pallas_call(
        functools.partial(back_kernel, n_phi, n_eta, n_hi),
        in_specs=[whole] * 7,
        out_specs=[whole] * 5,
        out_shape=[
            jax.ShapeDtypeStruct((n_edges, width), BF16),
            jax.ShapeDtypeStruct((n_edges, width), BF16),
            jax.ShapeDtypeStruct((n_in, hid), F32),
            jax.ShapeDtypeStruct((hid, width), F32),
            jax.ShapeDtypeStruct((1, hid), F32),
        ],
        scratch_shapes=[
            pltpu.VMEM(box, BF16),
            pltpu.VMEM((n_edges, wide), F32),
            pltpu.VMEM((n_plane,) + shard, BF16),
            pltpu.VMEM((2 * n_hi,) + shard[1:], BF16),
            pltpu.VMEM(shard, BF16),
            pltpu.VMEM((n_plane,) + shard, BF16),
            pltpu.VMEM((ndev, 1, hid), F32),
            each_dev, each_dev, grad_sems, grad_sems, each_dev, each_dev,
        ],
        compiler_params=remote(1),
        name="send_back",
    )(
        flat.reshape(n_phi, 1, slots // n_phi), near_sum, edges, cotangent, payload.reshape(box),
        grads.reshape((n_plane,) + shard), bias,
    )
    anywhere = pl.BlockSpec(memory_space=pl.ANY)
    new_edges, edge_grad, grad_first, grad_second, grad_bias = pl.pallas_call(
        hand_kernel,
        in_specs=[anywhere] * 5,
        out_specs=[anywhere] * 5,
        out_shape=[jax.ShapeDtypeStruct(o.shape, o.dtype) for o in outs],
        scratch_shapes=[pltpu.SemaphoreType.DMA((5,))],
        name="hand_over",
    )(*outs)
    return (new_edges, edge_grad, grad_first, grad_bias.reshape(hid), grad_second)


def solution(mesh):
    spec = P(AXES, None)
    in_specs = (spec, spec, P(AXES, None, None), spec, P(AXES), P(AXES), P(), P(), P())
    out_specs = (spec, spec, P(), P(), P())
    return jax.shard_map(local, mesh=mesh, in_specs=in_specs, out_specs=out_specs, check_vma=False)
```

```python
import functools

import jax
import jax.numpy as jnp
from jax import lax
from jax.experimental import pallas as pl
from jax.experimental.pallas import tpu as pltpu
from jax.sharding import PartitionSpec as P

AXES = ("phi", "eta")
F32 = jnp.float32
BF16 = jnp.bfloat16
I32 = jnp.int32
VMEM_LIMIT = 60 * 1024 * 1024
MESH = pl.DeviceIdType.MESH
ROWS = 256
ITEM = 128


def dot(a, b):
    return jnp.dot(a, b, preferred_element_type=F32)


def dot_nt(a, b):
    return lax.dot_general(a, b, (((1,), (1,)), ((), ())), preferred_element_type=F32)


def dot_tn(a, b):
    return lax.dot_general(a, b, (((0,), (0,)), ((), ())), preferred_element_type=F32)


def upright(idx):
    i, t = idx.shape
    return jnp.concatenate([jnp.broadcast_to(idx[u : u + 1], (128, t)).T for u in range(i)], axis=0)


def pick_upright(cols, n, start=0):
    lane = lax.broadcasted_iota(I32, (cols.shape[0], 128), 1)
    parts = [
        jnp.where(cols - (start + 128 * j) == lane, 1.0, 0.0).astype(BF16) for j in range(n // 128)
    ]
    return jnp.concatenate(parts, axis=1)


def flat_row(idx):
    return jnp.concatenate([idx[u : u + 1] for u in range(idx.shape[0])], axis=1)


def pick_cols(idx, n):
    row = lax.broadcasted_iota(I32, (n, idx.shape[1]), 0)
    return jnp.where(row == idx, 1.0, 0.0).astype(BF16)


def group_sort(x):
    g = x.shape[0]
    gb = g.bit_length() - 1
    n_bits = gb + 10
    lane = lax.broadcasted_iota(I32, (1, 8, 128), 2)
    sub = lax.broadcasted_iota(I32, (1, 8, 128), 1)
    grp = lax.broadcasted_iota(I32, (g, 8, 128), 0)

    def low(b):
        if b < gb:
            return (grp & (1 << b)) == 0
        if b < gb + 3:
            return (sub & (1 << (b - gb))) == 0
        return (lane & (1 << (b - gb - 3))) == 0

    for k in range(1, n_bits + 1):
        last = k == n_bits
        for j in range(k - 1, -1, -1):
            if last and j < gb + 3:
                break
            if j < gb:
                h = 1 << j
                split = (g // (2 * h), 2, h, 8, 128)
                y = x.reshape(split)
                a, b = y[:, 0], y[:, 1]
                small, large = jnp.minimum(a, b), jnp.maximum(a, b)
                up = low(k)
                if k < gb:
                    up = jnp.broadcast_to(up, (g, 8, 128)).reshape(split)[:, 0]
                else:
                    up = jnp.broadcast_to(up[None], a.shape)
                pair = [jnp.where(up, small, large), jnp.where(up, large, small)]
                x = jnp.stack(pair, axis=1).reshape(g, 8, 128)
            else:
                if j < gb + 3:
                    d, ax, size = 1 << (j - gb), 1, 8
                else:
                    d, ax, size = 1 << (j - gb - 3), 2, 128
                lo = low(j)
                if 2 * d == size:
                    other = pltpu.roll(x, d, ax)
                else:
                    other = jnp.where(
                        jnp.broadcast_to(lo, x.shape), pltpu.roll(x, size - d, ax), pltpu.roll(x, d, ax)
                    )
                take = lo if last else lo == low(k)
                x = jnp.where(
                    jnp.broadcast_to(take, x.shape), jnp.minimum(x, other), jnp.maximum(x, other)
                )
    return x


def place(n_phi, n_eta):
    phi = lax.axis_index("phi")
    eta = lax.axis_index("eta")
    return phi, eta, phi * n_eta + eta, n_phi * n_eta


def greet_all(n_eta, me, ndev):
    barrier = pltpu.get_barrier_semaphore()

    def greet(k, carry):
        peer = lax.rem(me + k, ndev)
        pl.semaphore_signal(
            barrier, inc=1, device_id=(peer // n_eta, lax.rem(peer, n_eta)), device_id_type=MESH
        )
        return carry

    lax.fori_loop(1, ndev, greet, 0)
    return barrier


def each(first, end, act):
    def body(k, carry):
        act(k)
        return carry

    lax.fori_loop(first, end, body, 0)


def slot_copy(n_phi, n_eta, k, src, dst, send_sem, recv_sem):
    phi, eta, me, ndev = place(n_phi, n_eta)
    to_phi, to_eta = lax.rem(phi + k // n_eta, n_phi), lax.rem(eta + lax.rem(k, n_eta), n_eta)
    return pltpu.make_async_remote_copy(
        src_ref=src.at[to_phi * n_eta + to_eta],
        dst_ref=dst.at[me],
        send_sem=send_sem.at[k],
        recv_sem=recv_sem.at[k],
        device_id=(to_phi, to_eta),
        device_id_type=MESH,
    )


def fused_kernel(
    n_phi, n_eta, n_hi, stride,
    rows_ref, count_ref, edges_ref, cot_ref, loc_ref, rem_ref, w1_ref, b1_ref, w2_ref,
    new_ref, grad_ref, g1_ref, g2_ref, gb_ref,
    outbox, inbox, flat, near_idx, rem_idx, keep, meta, meta_s, near, far, mdb, da, acc_r, pay, back_in,
    sums, acc_n, total, g1, g2, pack, plane_in, line_in, line_out, plane_out, biases,
    send_a, recv_a, send_s, recv_s, send_g, recv_g, send_b, recv_b, meta_sem,
):
    phi, eta, me, ndev = place(n_phi, n_eta)
    cap = rows_ref.shape[2]
    n_block, _, width = edges_ref.shape
    n_edges = n_block * ROWS
    wide = 2 * width
    n_in, hid = w1_ref.shape
    n_item = near_idx.shape[0]
    part = n_eta * cap
    bits = stride.bit_length() - 1
    barrier = greet_all(n_eta, me, ndev)
    out_copy = lambda k: slot_copy(n_phi, n_eta, k, outbox, inbox, send_a, recv_a)
    back_copy = lambda k: slot_copy(n_phi, n_eta, k, pay, back_in, send_s, recv_s)

    src = lax.broadcasted_iota(I32, (ndev, ndev), 0)
    dst = lax.broadcasted_iota(I32, (ndev, ndev), 1)
    counts = jnp.sum(jnp.where(src == dst, count_ref[...], 0), axis=1, keepdims=True)
    slot = lax.broadcasted_iota(I32, (ndev, cap), 1)
    live = jnp.where(slot < counts, rows_ref[0], -1)
    for d in range(ndev):
        e = d % n_eta
        flat[d // n_eta, :, e * cap : (e + 1) * cap] = live[d : d + 1, :]
    both = jnp.concatenate([edges_ref[...], cot_ref[...]], axis=2).reshape(n_edges, wide)
    for p in range(n_phi):
        picked = dot(pick_upright(upright(flat[p]), n_edges), both).astype(BF16)
        outbox[p * n_eta : (p + 1) * n_eta] = picked.reshape(n_eta, cap, wide)
    inbox[me] = outbox[me]
    pl.semaphore_wait(barrier, ndev - 1)
    each(1, ndev, lambda k: out_copy(k).start())

    key = group_sort(loc_ref[...] * stride + rem_ref[...])
    group = key.shape[0] * 8
    key = key.reshape(group, 128)
    per = ITEM // group
    n_tile = 128 // per
    ends = jnp.max(key, axis=0, keepdims=True) >> bits
    lane = lax.broadcasted_iota(I32, (n_item, 128), 1)
    item = lax.broadcasted_iota(I32, (n_item, 128), 0)

    def cut(item):
        over = (lane % per == per - 1) & (lane // per + ends // ROWS < item)
        tile = jnp.sum(jnp.where(over, 1, 0), axis=1, keepdims=True)
        return tile, jnp.minimum(item - tile, n_block - 1)

    tile, block = cut(item)
    keep[...] = jnp.where(block == cut(item - 1)[1], 1.0, 0.0)
    meta[:n_item] = block
    upto = jnp.sum(jnp.where(block <= lane, 1, 0), axis=0, keepdims=True) - 1
    meta[n_item:] = jnp.broadcast_to(upto, (meta.shape[0] - n_item, 128))
    to_scalar = pltpu.make_async_copy(meta, meta_s, meta_sem)
    to_scalar.start()
    by_group = key.T
    digits = [((by_group >> (8 * n)) & 255).astype(F32).astype(BF16) for n in range(3)]
    columns = []
    for u in range(per):
        mine = jnp.where(lane == tile * per + u, 1.0, 0.0).astype(BF16)
        columns.append(sum(dot(mine, digit) * float(1 << (8 * n)) for n, digit in enumerate(digits)))
    key = jnp.concatenate(columns, axis=1).astype(I32)
    row = (key >> bits) - block * ROWS
    inside = (row >= 0) & (row < ROWS) & (tile < n_tile)
    near_idx[...] = jnp.where(inside, row, -1)
    rem_idx[...] = jnp.where(inside, key & (stride - 1), -1)
    to_scalar.wait()

    def items(i, n):
        return pl.ds(pl.multiple_of(i * n, 8), n)

    def triplets(i, n):
        return pl.ds(pl.multiple_of(i * n * ITEM, ITEM), n * ITEM)

    def take_near(i):
        idx = near_idx[items(i, 8), :]
        parts = []
        for u in range(8):
            block = meta_s[i * 8 + u, 0]
            rows = jnp.concatenate([edges_ref[block], cot_ref[block]], axis=1)
            parts.append(dot(pick_upright(upright(idx[u : u + 1]), ROWS), rows).astype(BF16))
        near[triplets(i, 8), :] = jnp.concatenate(parts, axis=0)

    each(0, n_item // 8, take_near)

    def came_from(q):
        return lax.rem(phi + n_phi - q, n_phi)

    def arrived(box, q):
        return box[pl.ds(came_from(q) * n_eta, n_eta)].reshape(part, wide)

    each(1, (n_phi - 1) * n_eta, lambda k: out_copy(k).wait())
    last = n_phi - 1

    def take_far(i):
        cols = upright(rem_idx[items(i, 8), :])
        hot = [pick_upright(cols, part, came_from(q) * part) for q in range(last)]
        rows = [arrived(inbox, q) for q in range(last)]
        far[triplets(i, 8), :] = dot(
            jnp.concatenate(hot, axis=1), jnp.concatenate(rows, axis=0)
        ).astype(BF16)

    each(0, n_item // 8, take_far)
    each(last * n_eta, ndev, lambda k: out_copy(k).wait())

    g1[...] = jnp.zeros_like(g1)
    g2[...] = jnp.zeros_like(g2)
    biases[me] = jnp.zeros((1, hid), F32)

    def network(i):
        at = triplets(i, 8)
        hot = pick_upright(upright(rem_idx[items(i, 8), :]), part, came_from(last) * part)
        rest = dot(hot, arrived(inbox, last))
        outer = far[at, :].astype(F32) + rest
        a_b = near[at, :width]
        a = a_b.astype(F32)
        b = outer[:, :width]
        dm = (near[at, width:].astype(F32) + outer[:, width:]).astype(BF16)
        x = jnp.concatenate([a_b, b.astype(BF16), (a * b).astype(BF16)], axis=1)
        pre = dot(x, w1_ref[...]) + b1_ref[...]
        sig = 0.5 * jnp.tanh(0.5 * pre) + 0.5
        h = (pre * sig).astype(BF16)
        mdb[at, :width] = dot(h, w2_ref[...]).astype(BF16)
        dpre = dot_nt(dm, w2_ref[...]) * (sig * (1.0 + pre * (1.0 - sig)))
        dpre_b = dpre.astype(BF16)
        dx = dot_nt(dpre_b, w1_ref[...])
        dprod = dx[:, wide:]
        da[at, :] = (dx[:, :width] + dprod * b).astype(BF16)
        mdb[at, width:] = (dx[:, width:wide] + dprod * a).astype(BF16)
        g1[...] += dot_tn(x, dpre_b)
        g2[...] += dot_tn(h, dm)
        biases[me] += jnp.sum(dpre, axis=0, keepdims=True)

    each(0, n_item // 8, network)

    n_lo = n_eta // n_hi
    n_plane = n_phi * n_lo
    hi, lo = eta // n_lo, lax.rem(eta, n_lo)
    my_plane = phi * n_lo + lo

    def in_plane(k):
        other = lax.rem(my_plane + k, n_plane)
        return other, (other // n_lo, hi * n_lo + lax.rem(other, n_lo))

    def in_line(k):
        other = lax.rem(hi + k, n_hi)
        return other, (phi, other * n_lo + lo)

    def grad_copy(slot, src, dst, peer):
        return pltpu.make_async_remote_copy(
            src_ref=src, dst_ref=dst, send_sem=send_g.at[slot], recv_sem=recv_g.at[slot],
            device_id=peer, device_id_type=MESH,
        )

    def plane_reduce(k):
        other, peer = in_plane(k)
        return grad_copy(k, pack.at[other], plane_in.at[my_plane], peer)

    def line_reduce(k):
        other, peer = in_line(k)
        return grad_copy(n_plane + k, line_in.at[n_hi + other], line_in.at[hi], peer)

    def line_gather(k):
        other, peer = in_line(k)
        return grad_copy(n_plane + n_hi + k, line_out.at[hi], line_out.at[hi], peer)

    def plane_gather(k):
        other, peer = in_plane(k)
        return grad_copy(
            n_plane + 2 * n_hi + k, plane_out.at[my_plane], plane_out.at[my_plane], peer
        )

    def bias_copy(k):
        peer = lax.rem(me + k, ndev)
        return pltpu.make_async_remote_copy(
            src_ref=biases.at[me], dst_ref=biases.at[me], send_sem=send_b.at[k], recv_sem=recv_b.at[k],
            device_id=(peer // n_eta, lax.rem(peer, n_eta)), device_id_type=MESH,
        )

    def plane_start():
        second = [g2[k * width : (k + 1) * width, :] for k in range(hid // width)]
        values = jnp.concatenate([g1[...], jnp.concatenate(second, axis=1)], axis=0)
        pack[...] = values.astype(BF16).reshape(pack.shape)
        plane_in[my_plane] = pack[my_plane]
        each(1, n_plane, lambda k: plane_reduce(k).start())

    def plane_to_line():
        each(1, n_plane, lambda k: plane_reduce(k).wait())
        line_in[n_hi:] = jnp.sum(plane_in[...].astype(F32), axis=0).astype(BF16)
        line_in[hi] = line_in[n_hi + hi]
        each(1, n_hi, lambda k: line_reduce(k).start())

    def line_to_line():
        each(1, n_hi, lambda k: line_reduce(k).wait())
        line_out[hi] = jnp.sum(line_in[:n_hi].astype(F32), axis=0).astype(BF16)
        each(1, n_hi, lambda k: line_gather(k).start())

    def line_to_plane():
        each(1, n_hi, lambda k: line_gather(k).wait())
        plane_out[my_plane] = line_out[...]
        each(1, n_plane, lambda k: plane_gather(k).start())

    wide_n = 24 if n_item % 24 == 0 else 8

    def back(q):
        group_q = lax.rem(phi + q, n_phi)
        acc_r[...] = jnp.zeros_like(acc_r)

        def add_up(i):
            idx = flat_row(rem_idx[items(i, wide_n), :]) - group_q * part
            acc_r[...] += dot(pick_cols(idx, part), mdb[triplets(i, wide_n), :])

        each(0, n_item // wide_n, add_up)
        pay[pl.ds(group_q * n_eta, n_eta)] = acc_r[...].astype(BF16).reshape(n_eta, cap, wide)

    plane_start()
    back(0)
    back_in[me] = pay[me]
    each(1, n_eta, lambda k: back_copy(k).start())
    back(1)
    plane_to_line()
    each(n_eta, 2 * n_eta, lambda k: back_copy(k).start())
    for q in range(2, n_phi):
        back(q)
        if q == 2:
            line_to_line()
        each(q * n_eta, (q + 1) * n_eta, lambda k: back_copy(k).start())
        if q == 2:
            each(1, ndev, lambda k: bias_copy(k).start())

    acc_n[...] = jnp.zeros_like(acc_n)

    def add_near(i):
        idx = near_idx[items(i, 8), :]
        same8 = keep[items(i, 8), :]
        for u in range(8):
            w = i * 8 + u
            span = pl.ds(pl.multiple_of(w * ITEM, ITEM), ITEM)
            rows = jnp.concatenate([mdb[span, :width], da[span, :]], axis=1)
            same = jnp.concatenate([same8[u : u + 1]] * (wide // 128), axis=1)
            value = acc_n[...] * same + dot(pick_cols(idx[u : u + 1], ROWS), rows)
            acc_n[...] = value
            sums[w] = value

    each(0, n_item // 8, add_near)
    line_to_plane()
    for b in range(n_block):
        total[b * ROWS : (b + 1) * ROWS, :] = sums[meta_s[n_item, b]]

    for q in range(n_phi):
        each(max(q * n_eta, 1), (q + 1) * n_eta, lambda k: back_copy(k).wait())
        total[...] += dot(pick_cols(flat[came_from(q)], n_edges), arrived(back_in, q))

    old = edges_ref[...].astype(F32).reshape(n_edges, width)
    new_ref[...] = (old + total[:, :width]).astype(BF16)
    old = cot_ref[...].astype(F32).reshape(n_edges, width)
    grad_ref[...] = (old + total[:, width:]).astype(BF16)
    each(1, ndev, lambda k: bias_copy(k).wait())
    gb_ref[...] = jnp.sum(biases[...], axis=0)
    each(1, n_plane, lambda k: plane_gather(k).wait())
    values = plane_out[...].astype(F32).reshape(n_in + width, hid)
    g1_ref[...] = values[:n_in]
    for k in range(hid // width):
        g2_ref[k * width : (k + 1) * width, :] = values[n_in:, k * width : (k + 1) * width]


def hand_kernel(*refs):
    n = len(refs) // 2
    for i in range(n):
        refs[n + i][...] = refs[i][...]


def local(
    edges, cotangent, send_rows, send_count, trip_local, trip_remote, w_first, bias_first, w_second
):
    n_edges, width = edges.shape
    n_in, hid = w_first.shape
    n_phi, n_eta = lax.axis_size("phi"), lax.axis_size("eta")
    ndev = n_phi * n_eta
    cap = send_rows.shape[2]
    slots = ndev * cap
    n_trip = trip_local.shape[0]
    wide = 2 * width
    pack = n_in + width
    stride = 1 << (slots - 1).bit_length()
    n_item = -(-(n_trip // ITEM + n_edges // ROWS - 1) // 8) * 8
    padded = n_item * ITEM
    n_hi = 4 if n_eta % 4 == 0 else 1
    n_plane = ndev // n_hi
    shard = (n_hi, pack // ndev, hid)
    box = (ndev, cap, wide)
    part = n_eta * cap
    blocks = (n_edges // ROWS, ROWS, width)
    whole = pl.BlockSpec(memory_space=pltpu.VMEM)
    vmem = pltpu.VMEM
    each_dev = pltpu.SemaphoreType.DMA((ndev,))
    grad_sems = pltpu.SemaphoreType.DMA((2 * n_plane + 2 * n_hi,))
    outs = pl.pallas_call(
        functools.partial(fused_kernel, n_phi, n_eta, n_hi, stride),
        in_specs=[whole] * 9,
        out_specs=[whole] * 5,
        out_shape=[
            jax.ShapeDtypeStruct((n_edges, width), BF16),
            jax.ShapeDtypeStruct((n_edges, width), BF16),
            jax.ShapeDtypeStruct((n_in, hid), F32),
            jax.ShapeDtypeStruct((hid, width), F32),
            jax.ShapeDtypeStruct((1, hid), F32),
        ],
        scratch_shapes=[
            vmem(box, BF16),
            vmem(box, BF16),
            vmem((n_phi, 1, part), I32),
            vmem((n_item, ITEM), I32),
            vmem((n_item, ITEM), I32),
            vmem((n_item, 128), F32),
            vmem((n_item + 8, 128), I32),
            pltpu.SMEM((n_item + 8, 128), I32),
            vmem((padded, wide), BF16),
            vmem((padded, wide), BF16),
            vmem((padded, wide), BF16),
            vmem((padded, width), BF16),
            vmem((part, wide), F32),
            vmem(box, BF16),
            vmem(box, BF16),
            vmem((n_item, ROWS, wide), F32),
            vmem((ROWS, wide), F32),
            vmem((n_edges, wide), F32),
            vmem((n_in, hid), F32),
            vmem((hid, width), F32),
            vmem((n_plane,) + shard, BF16),
            vmem((n_plane,) + shard, BF16),
            vmem((2 * n_hi,) + shard[1:], BF16),
            vmem(shard, BF16),
            vmem((n_plane,) + shard, BF16),
            vmem((ndev, 1, hid), F32),
            each_dev, each_dev, each_dev, each_dev, grad_sems, grad_sems, each_dev, each_dev,
            pltpu.SemaphoreType.DMA,
        ],
        compiler_params=pltpu.CompilerParams(
            collective_id=0, has_side_effects=True, vmem_limit_bytes=VMEM_LIMIT
        ),
        name="triplet_section",
    )(
        send_rows, send_count, edges.reshape(blocks), cotangent.reshape(blocks),
        trip_local.reshape(n_trip // 1024, 8, 128), trip_remote.reshape(n_trip // 1024, 8, 128),
        w_first, bias_first.reshape(1, hid), w_second,
    )
    new_edges, edge_grad, grad_first, grad_second, grad_bias = pl.pallas_call(
        hand_kernel,
        in_specs=[whole] * 5,
        out_specs=[whole] * 5,
        out_shape=[jax.ShapeDtypeStruct(o.shape, o.dtype) for o in outs],
        name="hand_over",
    )(*outs)
    return (new_edges, edge_grad, grad_first, grad_bias.reshape(hid), grad_second)


def solution(mesh):
    spec = P(AXES, None)
    in_specs = (spec, spec, P(AXES, None, None), spec, P(AXES), P(AXES), P(), P(), P())
    out_specs = (spec, spec, P(), P(), P())
    return jax.shard_map(local, mesh=mesh, in_specs=in_specs, out_specs=out_specs, check_vma=False)
```

```python
import functools

import jax
import jax.numpy as jnp
from jax import lax
from jax.experimental import pallas as pl
from jax.experimental.pallas import tpu as pltpu
from jax.sharding import PartitionSpec as P

AXES = ("phi", "eta")
F32 = jnp.float32
BF16 = jnp.bfloat16
I32 = jnp.int32
VMEM_LIMIT = 60 * 1024 * 1024
MESH = pl.DeviceIdType.MESH
ROWS = 256
ITEM = 128
FAR, NET, BACK = 24, 8, 24
MASK = 6144
OUT_ORDER, BACK_ORDER = (2, 0, 1, 3), (2, 0, 1, 3)


def dot(a, b):
    return jnp.dot(a, b, preferred_element_type=F32)


def dot_nt(a, b):
    return lax.dot_general(a, b, (((1,), (1,)), ((), ())), preferred_element_type=F32)


def dot_tn(a, b):
    return lax.dot_general(a, b, (((0,), (0,)), ((), ())), preferred_element_type=F32)


def upright(idx):
    i, t = idx.shape
    return jnp.concatenate([jnp.broadcast_to(idx[u : u + 1], (128, t)).T for u in range(i)], axis=0)


def small(idx, top=256):
    return jnp.clip(idx, -1, top).astype(F32)


def pick_upright(idx, n):
    t = idx.size
    lane = lax.broadcasted_iota(I32, (t, 128), 1).astype(F32).astype(BF16)
    one, zero = jnp.ones((t, 128), BF16), jnp.zeros((t, 128), BF16)
    if n <= 256:
        cols = upright(small(idx)).astype(BF16)
        parts = [jnp.where(cols == lane + jnp.asarray(128 * j, BF16), one, zero) for j in range(n // 128)]
    else:
        low = upright((idx & 127).astype(F32)).astype(BF16)
        high = upright(jnp.clip(idx >> 7, -1, n // 128).astype(F32)).astype(BF16)
        hot = jnp.where(low == lane, one, zero)
        parts = [jnp.where(high == jnp.asarray(j, BF16), hot, zero) for j in range(n // 128)]
    return jnp.concatenate(parts, axis=1)


def pick_cols(idx, n):
    t = idx.shape[1]
    rows = min(n, 256)
    row = lax.broadcasted_iota(I32, (rows, t), 0).astype(F32).astype(BF16)
    one, zero = jnp.ones((rows, t), BF16), jnp.zeros((rows, t), BF16)

    def spread(x):
        part = jnp.broadcast_to(x, (16, t)).astype(BF16)
        return jnp.concatenate([part] * (rows // 16), axis=0)

    if n <= 256:
        return jnp.where(spread(small(idx)) == row, one, zero)
    hot = jnp.where(spread((idx & 255).astype(F32)) == row, one, zero)
    high = spread(jnp.clip(idx >> 8, -1, n // 256).astype(F32))
    return jnp.concatenate(
        [jnp.where(high == jnp.asarray(j, BF16), hot, zero) for j in range(n // 256)], axis=0
    )


def flat_row(idx):
    return jnp.concatenate([idx[u : u + 1] for u in range(idx.shape[0])], axis=1)


def pick_cols(idx, n):
    row = lax.broadcasted_iota(I32, (n, idx.shape[1]), 0)
    return jnp.where(row == idx, 1.0, 0.0).astype(BF16)


def group_sort(x):
    g = x.shape[0]
    gb = g.bit_length() - 1
    n_bits = gb + 10
    lane = lax.broadcasted_iota(I32, (1, 8, 128), 2)
    sub = lax.broadcasted_iota(I32, (1, 8, 128), 1)
    grp = lax.broadcasted_iota(I32, (g, 8, 128), 0)

    def low(b):
        if b < gb:
            return (grp & (1 << b)) == 0
        if b < gb + 3:
            return (sub & (1 << (b - gb))) == 0
        return (lane & (1 << (b - gb - 3))) == 0

    for k in range(1, n_bits + 1):
        last = k == n_bits
        for j in range(k - 1, -1, -1):
            if last and j < gb + 3:
                break
            if j < gb:
                h = 1 << j
                split = (g // (2 * h), 2, h, 8, 128)
                y = x.reshape(split)
                a, b = y[:, 0], y[:, 1]
                small, large = jnp.minimum(a, b), jnp.maximum(a, b)
                up = low(k)
                if k < gb:
                    up = jnp.broadcast_to(up, (g, 8, 128)).reshape(split)[:, 0]
                else:
                    up = jnp.broadcast_to(up[None], a.shape)
                pair = [jnp.where(up, small, large), jnp.where(up, large, small)]
                x = jnp.stack(pair, axis=1).reshape(g, 8, 128)
            else:
                if j < gb + 3:
                    d, ax, size = 1 << (j - gb), 1, 8
                else:
                    d, ax, size = 1 << (j - gb - 3), 2, 128
                lo = low(j)
                if 2 * d == size:
                    other = pltpu.roll(x, d, ax)
                else:
                    other = jnp.where(
                        jnp.broadcast_to(lo, x.shape), pltpu.roll(x, size - d, ax), pltpu.roll(x, d, ax)
                    )
                take = lo if last else lo == low(k)
                x = jnp.where(
                    jnp.broadcast_to(take, x.shape), jnp.minimum(x, other), jnp.maximum(x, other)
                )
    return x


def place(n_phi, n_eta):
    phi = lax.axis_index("phi")
    eta = lax.axis_index("eta")
    return phi, eta, phi * n_eta + eta, n_phi * n_eta


def greet_all(n_eta, me, ndev):
    barrier = pltpu.get_barrier_semaphore()

    def greet(k, carry):
        peer = lax.rem(me + k, ndev)
        pl.semaphore_signal(
            barrier, inc=1, device_id=(peer // n_eta, lax.rem(peer, n_eta)), device_id_type=MESH
        )
        return carry

    lax.fori_loop(1, ndev, greet, 0)
    return barrier


def each(first, end, act):
    def body(k, carry):
        act(k)
        return carry

    lax.fori_loop(first, end, body, 0)


def fused_kernel(
    n_phi, n_eta, n_hi, stride,
    rows_ref, count_ref, edges_ref, cot_ref, loc_ref, rem_ref, w1_ref, b1_ref, w2_ref,
    new_ref, grad_ref, g1_ref, g2_ref, gb_ref,
    outbox, inbox, flat, near_idx, rem_idx, keep, meta, meta_s, near, far, mdb, da, acc_r, pay, back_in,
    sums, total, g1, g2, pack, plane_in, line_in, line_out, plane_out, biases,
    send_a, recv_a, send_s, recv_s, send_g, recv_g, send_b, recv_b, meta_sem,
):
    phi, eta, me, ndev = place(n_phi, n_eta)
    cap = rows_ref.shape[2]
    n_block, _, width = edges_ref.shape
    n_edges = n_block * ROWS
    wide = 2 * width
    n_in, hid = w1_ref.shape
    n_item = near_idx.shape[0]
    part = ndev // n_hi * cap
    bits = stride.bit_length() - 1
    far_n, net_n, back_n = [n if n_item % n == 0 and n * part <= MASK else 8 for n in (FAR, NET, BACK)]
    n_lo = n_eta // n_hi
    n_plane = n_phi * n_lo
    hi, lo = eta // n_lo, lax.rem(eta, n_lo)
    my_plane = phi * n_lo + lo
    barrier = greet_all(n_eta, me, ndev)
    out_order, back_order = [[q for q in o if q < n_hi] for o in (OUT_ORDER, BACK_ORDER)]

    def plane_of(q):
        return hi ^ q

    def slot_copy(k, src, dst, send_sem, recv_sem):
        plane = plane_of(k // n_plane)
        other = lax.rem(my_plane + k, n_plane)
        return pltpu.make_async_remote_copy(
            src_ref=src.at[plane, other],
            dst_ref=dst.at[hi, my_plane],
            send_sem=send_sem.at[k],
            recv_sem=recv_sem.at[k],
            device_id=(other // n_lo, plane * n_lo + lax.rem(other, n_lo)),
            device_id_type=MESH,
        )

    out_copy = lambda k: slot_copy(k, outbox, inbox, send_a, recv_a)
    back_copy = lambda k: slot_copy(k, pay, back_in, send_s, recv_s)

    def copies(q, act):
        each(max(q * n_plane, 1), (q + 1) * n_plane, act)


    src = lax.broadcasted_iota(I32, (ndev, ndev), 0)
    dst = lax.broadcasted_iota(I32, (ndev, ndev), 1)
    counts = jnp.sum(jnp.where(src == dst, count_ref[...], 0), axis=1, keepdims=True)
    slot = lax.broadcasted_iota(I32, (ndev, cap), 1)
    live = jnp.where(slot < counts, rows_ref[0], -1)
    for d in range(ndev):
        p, e = d // n_eta, d % n_eta
        at = (p * n_lo + e % n_lo) * cap
        flat[e // n_lo, :, at : at + cap] = live[d : d + 1, :]
    both = jnp.concatenate([edges_ref[...], cot_ref[...]], axis=2).reshape(n_edges, wide)
    for q in out_order:
        plane = plane_of(q)
        picked = dot(pick_upright(flat[plane], n_edges), both).astype(BF16)
        outbox[plane] = picked.reshape(n_plane, cap, wide)
        if q == out_order[0]:
            pl.semaphore_wait(barrier, ndev - 1)
        copies(q, lambda k: out_copy(k).start())
    inbox[hi, my_plane] = outbox[hi, my_plane]

    source, slot = rem_ref[...] // cap, rem_ref[...] % cap
    s_phi, s_eta = source // n_eta, source % n_eta
    source = (s_eta // n_lo) * n_plane + s_phi * n_lo + s_eta % n_lo
    key = group_sort(loc_ref[...] * stride + source * cap + slot)
    group = key.shape[0] * 8
    key = key.reshape(group, 128)
    per = ITEM // group
    n_tile = 128 // per
    ends = jnp.max(key, axis=0, keepdims=True) >> bits
    lane = lax.broadcasted_iota(I32, (n_item, 128), 1)
    item = lax.broadcasted_iota(I32, (n_item, 128), 0)

    def cut(item):
        over = (lane % per == per - 1) & (lane // per + ends // ROWS < item)
        tile = jnp.sum(jnp.where(over, 1, 0), axis=1, keepdims=True)
        return tile, jnp.minimum(item - tile, n_block - 1)

    tile, block = cut(item)
    keep[...] = jnp.where(block == cut(item - 1)[1], 1.0, 0.0)
    meta[:n_item] = block
    upto = jnp.sum(jnp.where(block <= lane, 1, 0), axis=0, keepdims=True)
    meta[n_item:] = jnp.broadcast_to(upto, (meta.shape[0] - n_item, 128))
    to_scalar = pltpu.make_async_copy(meta, meta_s, meta_sem)
    to_scalar.start()
    by_group = key.T
    digits = [((by_group >> (8 * n)) & 255).astype(F32).astype(BF16) for n in range(3)]
    columns = []
    for u in range(per):
        mine = jnp.where(lane == tile * per + u, 1.0, 0.0).astype(BF16)
        columns.append(sum(dot(mine, digit) * float(1 << (8 * n)) for n, digit in enumerate(digits)))
    key = jnp.concatenate(columns, axis=1).astype(I32)
    row = (key >> bits) - block * ROWS
    inside = (row >= 0) & (row < ROWS) & (tile < n_tile)
    near_idx[...] = jnp.where(inside, row, -1)
    rem_idx[...] = jnp.where(inside, key & (stride - 1), -1)
    to_scalar.wait()

    def items(i, n):
        return pl.ds(pl.multiple_of(i * n, 8), n)

    def triplets(i, n):
        return pl.ds(pl.multiple_of(i * n * ITEM, ITEM), n * ITEM)

    def take_near(i):
        idx = near_idx[items(i, 8), :]
        parts = []
        for u in range(8):
            block = meta_s[i * 8 + u, 0]
            rows = jnp.concatenate([edges_ref[block], cot_ref[block]], axis=1)
            parts.append(dot(pick_upright(idx[u : u + 1], ROWS), rows).astype(BF16))
        near[triplets(i, 8), :] = jnp.concatenate(parts, axis=0)

    each(0, n_item // 8, take_near)

    def arrived(box, q):
        return box[plane_of(q)].reshape(part, wide)

    early, late = list(range(n_hi // 2)), list(range(n_hi // 2, n_hi))

    def take(qs, i, n):
        idx = rem_idx[items(i, n), :]
        hot = [pick_upright(idx - plane_of(q) * part, part) for q in qs]
        rows = [arrived(inbox, q) for q in qs]
        return dot(jnp.concatenate(hot, axis=1), jnp.concatenate(rows, axis=0)).astype(BF16)

    def take_far(i):
        far[triplets(i, far_n), :] = take(early, i, far_n)

    if early:
        for q in early:
            copies(q, lambda k: out_copy(k).wait())
        each(0, n_item // far_n, take_far)
    for q in late:
        copies(q, lambda k: out_copy(k).wait())

    g1[...] = jnp.zeros_like(g1)
    g2[...] = jnp.zeros_like(g2)
    biases[me] = jnp.zeros((1, hid), F32)

    w2_half = w2_ref[...] * jnp.asarray(0.5, BF16)
    w1_half = w1_ref[...] * jnp.asarray(0.5, BF16)
    b1_half = b1_ref[...] * 0.5

    def network(i):
        at = triplets(i, net_n)
        outer = take(late, i, net_n)
        if early:
            outer = far[at, :] + outer
        a, b = near[at, :width], outer[:, :width]
        dm = near[at, width:] + outer[:, width:]
        x = jnp.concatenate([a, b, a * b], axis=1)
        half = dot(x, w1_half) + b1_half
        twice_sig = jnp.tanh(half) + 1.0
        act = half * twice_sig
        h = act.astype(BF16)
        mdb[at, :width] = dot(h, w2_ref[...]).astype(BF16)
        dpre = dot_nt(dm, w2_half) * (twice_sig * (1.0 + (half + half - act)))
        dpre_b = dpre.astype(BF16)
        dx = dot_nt(dpre_b, w1_ref[...])
        dprod = dx[:, wide:]
        da[at, :] = (dx[:, :width] + dprod * b.astype(F32)).astype(BF16)
        mdb[at, width:] = (dx[:, width:wide] + dprod * a.astype(F32)).astype(BF16)
        g1[...] += dot_tn(x, dpre_b)
        g2[...] += dot_tn(h, dm)
        biases[me] += jnp.sum(dpre, axis=0, keepdims=True)

    each(0, n_item // net_n, network)

    def in_plane(k):
        other = lax.rem(my_plane + k, n_plane)
        return other, (other // n_lo, hi * n_lo + lax.rem(other, n_lo))

    def in_line(k):
        other = lax.rem(hi + k, n_hi)
        return other, (phi, other * n_lo + lo)

    def grad_copy(slot, src, dst, peer):
        return pltpu.make_async_remote_copy(
            src_ref=src, dst_ref=dst, send_sem=send_g.at[slot], recv_sem=recv_g.at[slot],
            device_id=peer, device_id_type=MESH,
        )

    def plane_reduce(k):
        other, peer = in_plane(k)
        return grad_copy(k, pack.at[other], plane_in.at[my_plane], peer)

    def line_reduce(k):
        other, peer = in_line(k)
        return grad_copy(n_plane + k, line_in.at[n_hi + other], line_in.at[hi], peer)

    def line_gather(k):
        other, peer = in_line(k)
        return grad_copy(n_plane + n_hi + k, line_out.at[hi], line_out.at[hi], peer)

    def plane_gather(k):
        other, peer = in_plane(k)
        return grad_copy(
            n_plane + 2 * n_hi + k, plane_out.at[my_plane], plane_out.at[my_plane], peer
        )

    def bias_copy(k):
        peer = lax.rem(me + k, ndev)
        return pltpu.make_async_remote_copy(
            src_ref=biases.at[me], dst_ref=biases.at[me], send_sem=send_b.at[k], recv_sem=recv_b.at[k],
            device_id=(peer // n_eta, lax.rem(peer, n_eta)), device_id_type=MESH,
        )

    def plane_start():
        second = [g2[k * width : (k + 1) * width, :] for k in range(hid // width)]
        values = jnp.concatenate([g1[...], jnp.concatenate(second, axis=1)], axis=0)
        pack[...] = values.astype(BF16).reshape(pack.shape)
        plane_in[my_plane] = pack[my_plane]
        each(1, n_plane, lambda k: plane_reduce(k).start())

    def plane_to_line():
        each(1, n_plane, lambda k: plane_reduce(k).wait())
        line_in[n_hi:] = jnp.sum(plane_in[...].astype(F32), axis=0).astype(BF16)
        line_in[hi] = line_in[n_hi + hi]
        each(1, n_hi, lambda k: line_reduce(k).start())

    def line_to_line():
        each(1, n_hi, lambda k: line_reduce(k).wait())
        line_out[hi] = jnp.sum(line_in[:n_hi].astype(F32), axis=0).astype(BF16)
        each(1, n_hi, lambda k: line_gather(k).start())

    def line_to_plane():
        each(1, n_hi, lambda k: line_gather(k).wait())
        plane_out[my_plane] = line_out[...]
        each(1, n_plane, lambda k: plane_gather(k).start())

    def back(q):
        plane = plane_of(q)
        acc_r[...] = jnp.zeros_like(acc_r)

        def add_up(i):
            idx = flat_row(rem_idx[items(i, back_n), :]) - plane * part
            acc_r[...] += dot(pick_cols(idx, part), mdb[triplets(i, back_n), :])

        each(0, n_item // back_n, add_up)
        pay[plane] = acc_r[...].astype(BF16).reshape(n_plane, cap, wide)

    plane_start()
    stages = [lambda: None, lambda: None, plane_to_line, line_to_line]
    for n, q in enumerate(back_order):
        back(q)
        if n < len(stages):
            stages[n]()
        copies(q, lambda k: back_copy(k).start())
    for stage in stages[len(back_order) :]:
        stage()
    back_in[hi, my_plane] = pay[hi, my_plane]
    each(1, ndev, lambda k: bias_copy(k).start())

    sums[0] = jnp.zeros(sums.shape[1:], F32)

    def add_near(i):
        idx = near_idx[items(i, 8), :]
        same8 = keep[items(i, 8), :]
        for u in range(8):
            w = i * 8 + u
            span = pl.ds(pl.multiple_of(w * ITEM, ITEM), ITEM)
            rows = jnp.concatenate([mdb[span, :width], da[span, :]], axis=1)
            same = jnp.concatenate([same8[u : u + 1]] * (wide // 128), axis=1)
            sums[w + 1] = sums[w] * same + dot(pick_cols(idx[u : u + 1], ROWS), rows)

    each(0, n_item // 8, add_near)
    line_to_plane()
    for b in range(n_block):
        total[b * ROWS : (b + 1) * ROWS, :] = sums[meta_s[n_item, b]]

    for q in range(n_hi):
        copies(q, lambda k: back_copy(k).wait())
        total[...] += dot(pick_cols(flat[plane_of(q)], n_edges), arrived(back_in, q))

    old = edges_ref[...].astype(F32).reshape(n_edges, width)
    new_ref[...] = (old + total[:, :width]).astype(BF16)
    old = cot_ref[...].astype(F32).reshape(n_edges, width)
    grad_ref[...] = (old + total[:, width:]).astype(BF16)
    each(1, ndev, lambda k: bias_copy(k).wait())
    gb_ref[...] = jnp.sum(biases[...], axis=0)
    each(1, n_plane, lambda k: plane_gather(k).wait())
    values = plane_out[...].astype(F32).reshape(n_in + width, hid)
    g1_ref[...] = values[:n_in]
    for k in range(hid // width):
        g2_ref[k * width : (k + 1) * width, :] = values[n_in:, k * width : (k + 1) * width]


def hand_kernel(*refs):
    n = len(refs) // 2
    for i in range(n):
        refs[n + i][...] = refs[i][...]


def local(
    edges, cotangent, send_rows, send_count, trip_local, trip_remote, w_first, bias_first, w_second
):
    n_edges, width = edges.shape
    n_in, hid = w_first.shape
    n_phi, n_eta = lax.axis_size("phi"), lax.axis_size("eta")
    ndev = n_phi * n_eta
    cap = send_rows.shape[2]
    slots = ndev * cap
    n_trip = trip_local.shape[0]
    wide = 2 * width
    pack = n_in + width
    stride = 1 << (slots - 1).bit_length()
    n_item = -(-(n_trip // ITEM + n_edges // ROWS - 1) // 8) * 8
    padded = n_item * ITEM
    n_hi = len(OUT_ORDER) if n_eta % len(OUT_ORDER) == 0 else 1
    n_plane = ndev // n_hi
    shard = (n_hi, pack // ndev, hid)
    box = (n_hi, n_plane, cap, wide)
    part = n_plane * cap
    blocks = (n_edges // ROWS, ROWS, width)
    whole = pl.BlockSpec(memory_space=pltpu.VMEM)
    vmem = pltpu.VMEM
    each_dev = pltpu.SemaphoreType.DMA((ndev,))
    grad_sems = pltpu.SemaphoreType.DMA((2 * n_plane + 2 * n_hi,))
    outs = pl.pallas_call(
        functools.partial(fused_kernel, n_phi, n_eta, n_hi, stride),
        in_specs=[whole] * 9,
        out_specs=[whole] * 5,
        out_shape=[
            jax.ShapeDtypeStruct((n_edges, width), BF16),
            jax.ShapeDtypeStruct((n_edges, width), BF16),
            jax.ShapeDtypeStruct((n_in, hid), F32),
            jax.ShapeDtypeStruct((hid, width), F32),
            jax.ShapeDtypeStruct((1, hid), F32),
        ],
        scratch_shapes=[
            vmem(box, BF16),
            vmem(box, BF16),
            vmem((n_hi, 1, part), I32),
            vmem((n_item, ITEM), I32),
            vmem((n_item, ITEM), I32),
            vmem((n_item, 128), F32),
            vmem((n_item + 8, 128), I32),
            pltpu.SMEM((n_item + 8, 128), I32),
            vmem((padded, wide), BF16),
            vmem((padded, wide), BF16),
            vmem((padded, wide), BF16),
            vmem((padded, width), BF16),
            vmem((part, wide), F32),
            vmem(box, BF16),
            vmem(box, BF16),
            vmem((n_item + 1, ROWS, wide), F32),
            vmem((n_edges, wide), F32),
            vmem((n_in, hid), F32),
            vmem((hid, width), F32),
            vmem((n_plane,) + shard, BF16),
            vmem((n_plane,) + shard, BF16),
            vmem((2 * n_hi,) + shard[1:], BF16),
            vmem(shard, BF16),
            vmem((n_plane,) + shard, BF16),
            vmem((ndev, 1, hid), F32),
            each_dev, each_dev, each_dev, each_dev, grad_sems, grad_sems, each_dev, each_dev,
            pltpu.SemaphoreType.DMA,
        ],
        compiler_params=pltpu.CompilerParams(
            collective_id=0, has_side_effects=True, vmem_limit_bytes=VMEM_LIMIT
        ),
        name="triplet_section",
    )(
        send_rows, send_count, edges.reshape(blocks), cotangent.reshape(blocks),
        trip_local.reshape(n_trip // 1024, 8, 128), trip_remote.reshape(n_trip // 1024, 8, 128),
        w_first, bias_first.reshape(1, hid), w_second,
    )
    new_edges, edge_grad, grad_first, grad_second, grad_bias = pl.pallas_call(
        hand_kernel,
        in_specs=[whole] * 5,
        out_specs=[whole] * 5,
        out_shape=[jax.ShapeDtypeStruct(o.shape, o.dtype) for o in outs],
        name="hand_over",
    )(*outs)
    return (new_edges, edge_grad, grad_first, grad_bias.reshape(hid), grad_second)


def solution(mesh):
    spec = P(AXES, None)
    in_specs = (spec, spec, P(AXES, None, None), spec, P(AXES), P(AXES), P(), P(), P())
    out_specs = (spec, spec, P(), P(), P())
    return jax.shard_map(local, mesh=mesh, in_specs=in_specs, out_specs=out_specs, check_vma=False)
```

```python
import functools

import jax
import jax.numpy as jnp
from jax import lax
from jax.experimental import pallas as pl
from jax.experimental.pallas import tpu as pltpu
from jax.sharding import PartitionSpec as P

AXES = ("phi", "eta")
F32 = jnp.float32
BF16 = jnp.bfloat16
I32 = jnp.int32
VMEM_LIMIT = 60 * 1024 * 1024
MESH = pl.DeviceIdType.MESH
ROWS = 256
ITEM = 128
FAR, NET, BACK = 24, 24, 24
MASK = 6144
OUT_ORDER, BACK_ORDER = (2, 0, 1, 3), (2, 0, 1, 3)


def dot(a, b):
    return jnp.dot(a, b, preferred_element_type=F32)


def dot_nt(a, b):
    return lax.dot_general(a, b, (((1,), (1,)), ((), ())), preferred_element_type=F32)


def dot_tn(a, b):
    return lax.dot_general(a, b, (((0,), (0,)), ((), ())), preferred_element_type=F32)


def upright(idx):
    i, t = idx.shape
    return jnp.concatenate([jnp.broadcast_to(idx[u : u + 1], (128, t)).T for u in range(i)], axis=0)


def small(idx, top=256):
    return jnp.clip(idx, -1, top).astype(F32)


def pick_upright(idx, n):
    t = idx.size
    lane = lax.broadcasted_iota(I32, (t, 128), 1).astype(F32).astype(BF16)
    one, zero = jnp.ones((t, 128), BF16), jnp.zeros((t, 128), BF16)
    if n <= 256:
        cols = upright(small(idx)).astype(BF16)
        parts = [jnp.where(cols == lane + jnp.asarray(128 * j, BF16), one, zero) for j in range(n // 128)]
    else:
        low = upright((idx & 127).astype(F32)).astype(BF16)
        high = upright(jnp.clip(idx >> 7, -1, n // 128).astype(F32)).astype(BF16)
        hot = jnp.where(low == lane, one, zero)
        parts = [jnp.where(high == jnp.asarray(j, BF16), hot, zero) for j in range(n // 128)]
    return jnp.concatenate(parts, axis=1)


def pick_cols(idx, n):
    t = idx.shape[1]
    rows = min(n, 256)
    row = lax.broadcasted_iota(I32, (rows, t), 0).astype(F32).astype(BF16)
    one, zero = jnp.ones((rows, t), BF16), jnp.zeros((rows, t), BF16)

    def spread(x):
        part = jnp.broadcast_to(x, (16, t)).astype(BF16)
        return jnp.concatenate([part] * (rows // 16), axis=0)

    if n <= 256:
        return jnp.where(spread(small(idx)) == row, one, zero)
    hot = jnp.where(spread((idx & 255).astype(F32)) == row, one, zero)
    high = spread(jnp.clip(idx >> 8, -1, n // 256).astype(F32))
    return jnp.concatenate(
        [jnp.where(high == jnp.asarray(j, BF16), hot, zero) for j in range(n // 256)], axis=0
    )


def flat_row(idx):
    return jnp.concatenate([idx[u : u + 1] for u in range(idx.shape[0])], axis=1)


def pick_cols(idx, n):
    row = lax.broadcasted_iota(I32, (n, idx.shape[1]), 0)
    return jnp.where(row == idx, 1.0, 0.0).astype(BF16)


def group_sort(x):
    g = x.shape[0]
    gb = g.bit_length() - 1
    n_bits = gb + 10
    lane = lax.broadcasted_iota(I32, (1, 8, 128), 2)
    sub = lax.broadcasted_iota(I32, (1, 8, 128), 1)
    grp = lax.broadcasted_iota(I32, (g, 8, 128), 0)

    def low(b):
        if b < gb:
            return (grp & (1 << b)) == 0
        if b < gb + 3:
            return (sub & (1 << (b - gb))) == 0
        return (lane & (1 << (b - gb - 3))) == 0

    for k in range(1, n_bits + 1):
        last = k == n_bits
        for j in range(k - 1, -1, -1):
            if last and j < gb + 3:
                break
            if j < gb:
                h = 1 << j
                split = (g // (2 * h), 2, h, 8, 128)
                y = x.reshape(split)
                a, b = y[:, 0], y[:, 1]
                small, large = jnp.minimum(a, b), jnp.maximum(a, b)
                up = low(k)
                if k < gb:
                    up = jnp.broadcast_to(up, (g, 8, 128)).reshape(split)[:, 0]
                else:
                    up = jnp.broadcast_to(up[None], a.shape)
                pair = [jnp.where(up, small, large), jnp.where(up, large, small)]
                x = jnp.stack(pair, axis=1).reshape(g, 8, 128)
            else:
                if j < gb + 3:
                    d, ax, size = 1 << (j - gb), 1, 8
                else:
                    d, ax, size = 1 << (j - gb - 3), 2, 128
                lo = low(j)
                if 2 * d == size:
                    other = pltpu.roll(x, d, ax)
                else:
                    other = jnp.where(
                        jnp.broadcast_to(lo, x.shape), pltpu.roll(x, size - d, ax), pltpu.roll(x, d, ax)
                    )
                take = lo if last else lo == low(k)
                x = jnp.where(
                    jnp.broadcast_to(take, x.shape), jnp.minimum(x, other), jnp.maximum(x, other)
                )
    return x


def place(n_phi, n_eta):
    phi = lax.axis_index("phi")
    eta = lax.axis_index("eta")
    return phi, eta, phi * n_eta + eta, n_phi * n_eta


def greet_all(n_eta, me, ndev):
    barrier = pltpu.get_barrier_semaphore()

    def greet(k, carry):
        peer = lax.rem(me + k, ndev)
        pl.semaphore_signal(
            barrier, inc=1, device_id=(peer // n_eta, lax.rem(peer, n_eta)), device_id_type=MESH
        )
        return carry

    lax.fori_loop(1, ndev, greet, 0)
    return barrier


def each(first, end, act):
    def body(k, carry):
        act(k)
        return carry

    lax.fori_loop(first, end, body, 0)


def fused_kernel(
    n_phi, n_eta, n_hi, stride,
    rows_ref, count_ref, edges_ref, cot_ref, loc_ref, rem_ref, w1_ref, b1_ref, w2_ref,
    new_ref, grad_ref, g1_ref, g2_ref, gb_ref,
    outbox, inbox, flat, near_idx, rem_idx, keep, meta, meta_s, near, far, mdb, da, acc_r, pay, back_in,
    sums, total, g1, g2, pack, plane_in, line_in, line_out, plane_out, biases,
    send_a, recv_a, send_s, recv_s, send_g, recv_g, send_b, recv_b, meta_sem,
):
    phi, eta, me, ndev = place(n_phi, n_eta)
    cap = rows_ref.shape[2]
    n_block, _, width = edges_ref.shape
    n_edges = n_block * ROWS
    wide = 2 * width
    n_in, hid = w1_ref.shape
    n_item = near_idx.shape[0]
    part = ndev // n_hi * cap
    bits = stride.bit_length() - 1
    far_n, net_n, back_n = [n if n_item % n == 0 and n * part <= MASK else 8 for n in (FAR, NET, BACK)]
    n_lo = n_eta // n_hi
    n_plane = n_phi * n_lo
    hi, lo = eta // n_lo, lax.rem(eta, n_lo)
    my_plane = phi * n_lo + lo
    barrier = greet_all(n_eta, me, ndev)
    out_order, back_order = [[q for q in o if q < n_hi] for o in (OUT_ORDER, BACK_ORDER)]

    def plane_of(q):
        return hi ^ q

    def slot_copy(k, src, dst, send_sem, recv_sem):
        plane = plane_of(k // n_plane)
        other = lax.rem(my_plane + k, n_plane)
        return pltpu.make_async_remote_copy(
            src_ref=src.at[plane, other],
            dst_ref=dst.at[hi, my_plane],
            send_sem=send_sem.at[k],
            recv_sem=recv_sem.at[k],
            device_id=(other // n_lo, plane * n_lo + lax.rem(other, n_lo)),
            device_id_type=MESH,
        )

    out_copy = lambda k: slot_copy(k, outbox, inbox, send_a, recv_a)
    back_copy = lambda k: slot_copy(k, pay, back_in, send_s, recv_s)

    def copies(q, act):
        each(max(q * n_plane, 1), (q + 1) * n_plane, act)


    src = lax.broadcasted_iota(I32, (ndev, ndev), 0)
    dst = lax.broadcasted_iota(I32, (ndev, ndev), 1)
    counts = jnp.sum(jnp.where(src == dst, count_ref[...], 0), axis=1, keepdims=True)
    slot = lax.broadcasted_iota(I32, (ndev, cap), 1)
    live = jnp.where(slot < counts, rows_ref[0], -1)
    for d in range(ndev):
        p, e = d // n_eta, d % n_eta
        at = (p * n_lo + e % n_lo) * cap
        flat[e // n_lo, :, at : at + cap] = live[d : d + 1, :]
    both = jnp.concatenate([edges_ref[...], cot_ref[...]], axis=2).reshape(n_edges, wide)
    for q in out_order:
        plane = plane_of(q)
        picked = dot(pick_upright(flat[plane], n_edges), both).astype(BF16)
        outbox[plane] = picked.reshape(n_plane, cap, wide)
        if q == out_order[0]:
            pl.semaphore_wait(barrier, ndev - 1)
        copies(q, lambda k: out_copy(k).start())
    inbox[hi, my_plane] = outbox[hi, my_plane]

    source, slot = rem_ref[...] // cap, rem_ref[...] % cap
    s_phi, s_eta = source // n_eta, source % n_eta
    source = (s_eta // n_lo) * n_plane + s_phi * n_lo + s_eta % n_lo
    key = group_sort(loc_ref[...] * stride + source * cap + slot)
    group = key.shape[0] * 8
    key = key.reshape(group, 128)
    per = ITEM // group
    n_tile = 128 // per
    ends = jnp.max(key, axis=0, keepdims=True) >> bits
    lane = lax.broadcasted_iota(I32, (n_item, 128), 1)
    item = lax.broadcasted_iota(I32, (n_item, 128), 0)

    def cut(item):
        over = (lane % per == per - 1) & (lane // per + ends // ROWS < item)
        tile = jnp.sum(jnp.where(over, 1, 0), axis=1, keepdims=True)
        return tile, jnp.minimum(item - tile, n_block - 1)

    tile, block = cut(item)
    keep[...] = jnp.where(block == cut(item - 1)[1], 1.0, 0.0)
    meta[:n_item] = block
    upto = jnp.sum(jnp.where(block <= lane, 1, 0), axis=0, keepdims=True)
    meta[n_item:] = jnp.broadcast_to(upto, (meta.shape[0] - n_item, 128))
    to_scalar = pltpu.make_async_copy(meta, meta_s, meta_sem)
    to_scalar.start()
    by_group = key.T
    digits = [((by_group >> (8 * n)) & 255).astype(F32).astype(BF16) for n in range(3)]
    columns = []
    for u in range(per):
        mine = jnp.where(lane == tile * per + u, 1.0, 0.0).astype(BF16)
        columns.append(sum(dot(mine, digit) * float(1 << (8 * n)) for n, digit in enumerate(digits)))
    key = jnp.concatenate(columns, axis=1).astype(I32)
    row = (key >> bits) - block * ROWS
    inside = (row >= 0) & (row < ROWS) & (tile < n_tile)
    near_idx[...] = jnp.where(inside, row, -1)
    rem_idx[...] = jnp.where(inside, key & (stride - 1), -1)
    to_scalar.wait()

    def items(i, n):
        return pl.ds(pl.multiple_of(i * n, 8), n)

    def triplets(i, n):
        return pl.ds(pl.multiple_of(i * n * ITEM, ITEM), n * ITEM)

    def take_near(i):
        idx = near_idx[items(i, 8), :]
        parts = []
        for u in range(8):
            block = meta_s[i * 8 + u, 0]
            rows = jnp.concatenate([edges_ref[block], cot_ref[block]], axis=1)
            parts.append(dot(pick_upright(idx[u : u + 1], ROWS), rows).astype(BF16))
        near[triplets(i, 8), :] = jnp.concatenate(parts, axis=0)

    each(0, n_item // 8, take_near)

    def arrived(box, q):
        return box[plane_of(q)].reshape(part, wide)

    early, late = list(range(n_hi // 2)), list(range(n_hi // 2, n_hi))

    def take(qs, i, n):
        idx = rem_idx[items(i, n), :]
        hot = [pick_upright(idx - plane_of(q) * part, part) for q in qs]
        rows = [arrived(inbox, q) for q in qs]
        return dot(jnp.concatenate(hot, axis=1), jnp.concatenate(rows, axis=0)).astype(BF16)

    def take_far(i):
        far[triplets(i, far_n), :] = take(early, i, far_n)

    if early:
        for q in early:
            copies(q, lambda k: out_copy(k).wait())
        each(0, n_item // far_n, take_far)
    for q in late:
        copies(q, lambda k: out_copy(k).wait())

    g1[...] = jnp.zeros_like(g1)
    g2[...] = jnp.zeros_like(g2)
    biases[me] = jnp.zeros((1, hid), F32)

    w2_half = w2_ref[...] * jnp.asarray(0.5, BF16)
    w1_half = w1_ref[...] * jnp.asarray(0.5, BF16)
    b1_half = b1_ref[...] * 0.5

    def network(i):
        at = triplets(i, net_n)
        outer = take(late, i, net_n)
        if early:
            outer = far[at, :] + outer
        a, b = near[at, :width], outer[:, :width]
        dm = near[at, width:] + outer[:, width:]
        x = jnp.concatenate([a, b, a * b], axis=1)
        half = dot(x, w1_half) + b1_half
        twice_sig = jnp.tanh(half) + 1.0
        act = half * twice_sig
        h = act.astype(BF16)
        mdb[at, :width] = dot(h, w2_ref[...]).astype(BF16)
        dpre = dot_nt(dm, w2_half) * (twice_sig * (1.0 + (half + half - act)))
        dpre_b = dpre.astype(BF16)
        dx = dot_nt(dpre_b, w1_ref[...])
        dprod = dx[:, wide:]
        da[at, :] = (dx[:, :width] + dprod * b.astype(F32)).astype(BF16)
        mdb[at, width:] = (dx[:, width:wide] + dprod * a.astype(F32)).astype(BF16)
        g1[...] += dot_tn(x, dpre_b)
        g2[...] += dot_tn(h, dm)
        biases[me] += jnp.sum(dpre, axis=0, keepdims=True)

    each(0, n_item // net_n, network)

    def in_plane(k):
        other = lax.rem(my_plane + k, n_plane)
        return other, (other // n_lo, hi * n_lo + lax.rem(other, n_lo))

    def in_line(k):
        other = lax.rem(hi + k, n_hi)
        return other, (phi, other * n_lo + lo)

    def grad_copy(slot, src, dst, peer):
        return pltpu.make_async_remote_copy(
            src_ref=src, dst_ref=dst, send_sem=send_g.at[slot], recv_sem=recv_g.at[slot],
            device_id=peer, device_id_type=MESH,
        )

    def plane_reduce(k):
        other, peer = in_plane(k)
        return grad_copy(k, pack.at[other], plane_in.at[my_plane], peer)

    def line_reduce(k):
        other, peer = in_line(k)
        return grad_copy(n_plane + k, line_in.at[n_hi + other], line_in.at[hi], peer)

    def line_gather(k):
        other, peer = in_line(k)
        return grad_copy(n_plane + n_hi + k, line_out.at[hi], line_out.at[hi], peer)

    def plane_gather(k):
        other, peer = in_plane(k)
        return grad_copy(
            n_plane + 2 * n_hi + k, plane_out.at[my_plane], plane_out.at[my_plane], peer
        )

    def bias_copy(k):
        peer = lax.rem(me + k, ndev)
        return pltpu.make_async_remote_copy(
            src_ref=biases.at[me], dst_ref=biases.at[me], send_sem=send_b.at[k], recv_sem=recv_b.at[k],
            device_id=(peer // n_eta, lax.rem(peer, n_eta)), device_id_type=MESH,
        )

    def plane_start():
        second = [g2[k * width : (k + 1) * width, :] for k in range(hid // width)]
        values = jnp.concatenate([g1[...], jnp.concatenate(second, axis=1)], axis=0)
        pack[...] = values.astype(BF16).reshape(pack.shape)
        plane_in[my_plane] = pack[my_plane]
        each(1, n_plane, lambda k: plane_reduce(k).start())

    def plane_to_line():
        each(1, n_plane, lambda k: plane_reduce(k).wait())
        line_in[n_hi:] = jnp.sum(plane_in[...].astype(F32), axis=0).astype(BF16)
        line_in[hi] = line_in[n_hi + hi]
        each(1, n_hi, lambda k: line_reduce(k).start())

    def line_to_line():
        each(1, n_hi, lambda k: line_reduce(k).wait())
        line_out[hi] = jnp.sum(line_in[:n_hi].astype(F32), axis=0).astype(BF16)
        each(1, n_hi, lambda k: line_gather(k).start())

    def line_to_plane():
        each(1, n_hi, lambda k: line_gather(k).wait())
        plane_out[my_plane] = line_out[...]
        each(1, n_plane, lambda k: plane_gather(k).start())

    def back(q):
        plane = plane_of(q)
        acc_r[...] = jnp.zeros_like(acc_r)

        def add_up(i):
            idx = flat_row(rem_idx[items(i, back_n), :]) - plane * part
            acc_r[...] += dot(pick_cols(idx, part), mdb[triplets(i, back_n), :])

        each(0, n_item // back_n, add_up)
        pay[plane] = acc_r[...].astype(BF16).reshape(n_plane, cap, wide)

    plane_start()
    stages = [lambda: None, lambda: None, plane_to_line, line_to_line]
    for n, q in enumerate(back_order):
        back(q)
        if n < len(stages):
            stages[n]()
        copies(q, lambda k: back_copy(k).start())
    for stage in stages[len(back_order) :]:
        stage()
    back_in[hi, my_plane] = pay[hi, my_plane]
    each(1, ndev, lambda k: bias_copy(k).start())

    sums[0] = jnp.zeros(sums.shape[1:], F32)

    def add_near(i):
        idx = near_idx[items(i, 8), :]
        same8 = keep[items(i, 8), :]
        for u in range(8):
            w = i * 8 + u
            span = pl.ds(pl.multiple_of(w * ITEM, ITEM), ITEM)
            rows = jnp.concatenate([mdb[span, :width], da[span, :]], axis=1)
            same = jnp.concatenate([same8[u : u + 1]] * (wide // 128), axis=1)
            sums[w + 1] = sums[w] * same + dot(pick_cols(idx[u : u + 1], ROWS), rows)

    each(0, n_item // 8, add_near)
    line_to_plane()
    for b in range(n_block):
        total[b * ROWS : (b + 1) * ROWS, :] = sums[meta_s[n_item, b]]

    for q in range(n_hi):
        copies(q, lambda k: back_copy(k).wait())
        total[...] += dot(pick_cols(flat[plane_of(q)], n_edges), arrived(back_in, q))

    old = edges_ref[...].astype(F32).reshape(n_edges, width)
    new_ref[...] = (old + total[:, :width]).astype(BF16)
    old = cot_ref[...].astype(F32).reshape(n_edges, width)
    grad_ref[...] = (old + total[:, width:]).astype(BF16)
    each(1, ndev, lambda k: bias_copy(k).wait())
    gb_ref[...] = jnp.sum(biases[...], axis=0)
    each(1, n_plane, lambda k: plane_gather(k).wait())
    values = plane_out[...].astype(F32).reshape(n_in + width, hid)
    g1_ref[...] = values[:n_in]
    for k in range(hid // width):
        g2_ref[k * width : (k + 1) * width, :] = values[n_in:, k * width : (k + 1) * width]


def hand_kernel(*refs):
    n = len(refs) // 2
    for i in range(n):
        refs[n + i][...] = refs[i][...]


def local(
    edges, cotangent, send_rows, send_count, trip_local, trip_remote, w_first, bias_first, w_second
):
    n_edges, width = edges.shape
    n_in, hid = w_first.shape
    n_phi, n_eta = lax.axis_size("phi"), lax.axis_size("eta")
    ndev = n_phi * n_eta
    cap = send_rows.shape[2]
    slots = ndev * cap
    n_trip = trip_local.shape[0]
    wide = 2 * width
    pack = n_in + width
    stride = 1 << (slots - 1).bit_length()
    n_item = -(-(n_trip // ITEM + n_edges // ROWS - 1) // 8) * 8
    padded = n_item * ITEM
    n_hi = len(OUT_ORDER) if n_eta % len(OUT_ORDER) == 0 else 1
    n_plane = ndev // n_hi
    shard = (n_hi, pack // ndev, hid)
    box = (n_hi, n_plane, cap, wide)
    part = n_plane * cap
    blocks = (n_edges // ROWS, ROWS, width)
    whole = pl.BlockSpec(memory_space=pltpu.VMEM)
    vmem = pltpu.VMEM
    each_dev = pltpu.SemaphoreType.DMA((ndev,))
    grad_sems = pltpu.SemaphoreType.DMA((2 * n_plane + 2 * n_hi,))
    outs = pl.pallas_call(
        functools.partial(fused_kernel, n_phi, n_eta, n_hi, stride),
        in_specs=[whole] * 9,
        out_specs=[whole] * 5,
        out_shape=[
            jax.ShapeDtypeStruct((n_edges, width), BF16),
            jax.ShapeDtypeStruct((n_edges, width), BF16),
            jax.ShapeDtypeStruct((n_in, hid), F32),
            jax.ShapeDtypeStruct((hid, width), F32),
            jax.ShapeDtypeStruct((1, hid), F32),
        ],
        scratch_shapes=[
            vmem(box, BF16),
            vmem(box, BF16),
            vmem((n_hi, 1, part), I32),
            vmem((n_item, ITEM), I32),
            vmem((n_item, ITEM), I32),
            vmem((n_item, 128), F32),
            vmem((n_item + 8, 128), I32),
            pltpu.SMEM((n_item + 8, 128), I32),
            vmem((padded, wide), BF16),
            vmem((padded, wide), BF16),
            vmem((padded, wide), BF16),
            vmem((padded, width), BF16),
            vmem((part, wide), F32),
            vmem(box, BF16),
            vmem(box, BF16),
            vmem((n_item + 1, ROWS, wide), F32),
            vmem((n_edges, wide), F32),
            vmem((n_in, hid), F32),
            vmem((hid, width), F32),
            vmem((n_plane,) + shard, BF16),
            vmem((n_plane,) + shard, BF16),
            vmem((2 * n_hi,) + shard[1:], BF16),
            vmem(shard, BF16),
            vmem((n_plane,) + shard, BF16),
            vmem((ndev, 1, hid), F32),
            each_dev, each_dev, each_dev, each_dev, grad_sems, grad_sems, each_dev, each_dev,
            pltpu.SemaphoreType.DMA,
        ],
        compiler_params=pltpu.CompilerParams(
            collective_id=0, has_side_effects=True, vmem_limit_bytes=VMEM_LIMIT
        ),
        name="triplet_section",
    )(
        send_rows, send_count, edges.reshape(blocks), cotangent.reshape(blocks),
        trip_local.reshape(n_trip // 1024, 8, 128), trip_remote.reshape(n_trip // 1024, 8, 128),
        w_first, bias_first.reshape(1, hid), w_second,
    )
    new_edges, edge_grad, grad_first, grad_second, grad_bias = pl.pallas_call(
        hand_kernel,
        in_specs=[whole] * 5,
        out_specs=[whole] * 5,
        out_shape=[jax.ShapeDtypeStruct(o.shape, o.dtype) for o in outs],
        name="hand_over",
    )(*outs)
    return (new_edges, edge_grad, grad_first, grad_bias.reshape(hid), grad_second)


def solution(mesh):
    spec = P(AXES, None)
    in_specs = (spec, spec, P(AXES, None, None), spec, P(AXES), P(AXES), P(), P(), P())
    out_specs = (spec, spec, P(), P(), P())
    return jax.shard_map(local, mesh=mesh, in_specs=in_specs, out_specs=out_specs, check_vma=False)
```
